512 devices in a mesh: sector: 16 (over y, x), dom: 32 (over z, core).
Axes of the slice: x: 4, y: 4, z: 16, core: 2. Of those that a mesh axis runs over, the one named last changes fastest.
Arguments:
- strain_map: float32 [36, 131072], P(None, ('sector', 'dom')), may hold values from -1.75 to 1.75
- corner_nodes: int32 [4, 131072], P(None, ('sector', 'dom')), may hold values from 0 to 10239, as said below
- counts: int32 [512], P(('sector', 'dom')), may hold values from 64 to 256, as said below
- seam_nodes: int32 [16, 2048], P('sector'), may hold values from 0 to 8191
- velocity: float32 [3, 131072], P(None, ('sector', 'dom')), may hold values from -6 to 6
- dual_state: float32 [3, 131072], P(None, ('sector', 'dom')), may hold values from -6 to 6
- nodal_load: float32 [3, 131072], P(None, ('sector', 'dom')), may hold values from -6 to 6
- mobility: float32 [131072], P(('sector', 'dom')), may hold values from 0.1 to 0.5
- past_dual: float32 [8, 3, 131072], P(None, None, ('sector', 'dom')), may hold values from -6 to 6
- past_dual_gap: float32 [8, 3, 131072], P(None, None, ('sector', 'dom')), may hold values from -12 to 12
- past_velocity: float32 [8, 3, 131072], P(None, None, ('sector', 'dom')), may hold values from -6 to 6
- past_velocity_gap: float32 [8, 3, 131072], P(None, None, ('sector', 'dom')), may hold values from -12 to 12
Outputs:
- new_velocity: float32 [3, 131072], P(None, ('sector', 'dom'))
- new_dual: float32 [3, 131072], P(None, ('sector', 'dom'))
The draws below stay inside these ranges and needn't reach their ends.
Inputs may be any that keep to these rules, and one draw needn't show every extreme that they name: `counts`: each block has between 64 and 256 live elements; some block is full and some has exactly the least. `corner_nodes`: an element of block d of a sector (d = its slot's block index along dom) names either a seam position (8192 and up) or a node from d * 256 - 32 to (d + 1) * 256 + 31, within 0 to 8191; both ends of that range are named in every draw where they exist.
All inputs are finite; a program needn't handle non-finite values.
Results may differ from the reference program's by a relative error of at most 0.0003.
Values sent between devices are 32-bit elements; how exact they have to be, the bound alone decides.
A program may use at most 64 MiB of HBM per device.

```python
import math
import jax
import jax.numpy as jnp
from jax import lax

E_DEV = 256
SEAM = 2048
ITERS = 2
DEPTH = 8
BAND = 32
SECTORS = 16
BLOCKS = 512
ESEC = 8192
NODES_SEC = 8192
NREF = 10240
ELEMS = 131072
NODES = 131072


def regional_gap(key, columns):
    first = jax.random.fold_in(key, 0)
    base = jax.random.normal(first, (DEPTH, 3, columns), jnp.float32)
    base = jnp.clip(base, -6.0, 6.0)
    position = jnp.arange(columns, dtype=jnp.float32)[None, None, :] / columns
    position = position + jnp.arange(DEPTH, dtype=jnp.float32)[:, None, None] / DEPTH
    fraction = jnp.mod(position, 1.0)
    return 0.2 * jnp.power(10.0, fraction) * base


def draw_past_dual_gap(key, part):
    return regional_gap(jax.random.fold_in(key, 11), ELEMS)


def draw_past_velocity_gap(key, part):
    return regional_gap(jax.random.fold_in(key, 23), NODES)


def draw_counts(key, part):
    first, second = jax.random.split(jax.random.fold_in(key, 37))
    values = jax.random.randint(first, (BLOCKS,), E_DEV // 4, E_DEV + 1, dtype=jnp.int32)
    order = jax.random.permutation(second, BLOCKS)
    values = values.at[order[0]].set(E_DEV)
    values = values.at[order[1]].set(E_DEV // 4)
    return values.astype(jnp.int32)


def draw_corner_nodes(key, part):
    keys = jax.random.split(jax.random.fold_in(key, 53), 4)
    elem_index = jnp.arange(ELEMS, dtype=jnp.int32)
    blocks_sec = ESEC // E_DEV
    block_pos = elem_index // E_DEV % blocks_sec
    slot = elem_index % E_DEV
    kind = jax.random.randint(keys[0], (4, ELEMS), 0, 20, dtype=jnp.int32)
    own = block_pos[None, :] * E_DEV + jax.random.randint(keys[1], (4, ELEMS), 0, E_DEV, dtype=jnp.int32)
    offset = jax.random.randint(keys[2], (4, ELEMS), 0, BAND, dtype=jnp.int32)
    left = block_pos[None, :] * E_DEV - 1 - offset
    right = (block_pos[None, :] + 1) * E_DEV + offset
    seam = NODES_SEC + jax.random.randint(keys[3], (4, ELEMS), 0, SEAM, dtype=jnp.int32)
    left = jnp.where(left >= 0, left, own)
    right = jnp.where(right < NODES_SEC, right, own)
    chosen = jnp.where(kind < 16, own, jnp.where(kind == 16, left, jnp.where(kind == 17, right, seam)))
    far_right = (block_pos + 1) * E_DEV + BAND - 1
    far_left = block_pos * E_DEV - BAND
    row_one = jnp.where((slot == 1) & (far_right < NODES_SEC), far_right, chosen[1])
    row_two = jnp.where((slot == 2) & (far_left >= 0), far_left, chosen[2])
    chosen = chosen.at[1].set(row_one).at[2].set(row_two)
    chosen = chosen.at[0, 0].set(0).at[0, ELEMS - 1].set(NREF - 1)
    return chosen.astype(jnp.int32)


def set_ends(array, own_key, low, high):
    extent = array.shape
    index_at = [jax.random.randint(jax.random.fold_in(own_key, axis), (), 0, extent[axis]) for axis in range(len(extent))]
    array = array.at[tuple(index_at)].set(low)
    longest = extent.index(max(extent))
    index_at[longest] = (index_at[longest] + 1) % extent[longest]
    return array.at[tuple(index_at)].set(high)


def shard_levels(stream_key, shape, pieces, low, high):
    factor_of, own = 1.0, jax.random.fold_in(stream_key, 6)
    for dim, parts in pieces:
        draws = jnp.exp(jax.random.uniform(jax.random.fold_in(own, dim), (parts,), jnp.float32, low / len(pieces), high / len(pieces)))
        factor_of = factor_of * jnp.repeat(draws, shape[dim] // parts).reshape([-1 if axis == dim else 1 for axis in range(len(shape))])
    return factor_of


def normal_values(own_key, extent, scale, most, shards=(), held_as=jnp.bfloat16):
    values = jax.random.normal(own_key, extent, jnp.float32) * scale
    if len(shards) > 0:
        values = shard_levels(own_key, extent, shards, -0.22, 0.18) * values
    return jnp.clip(values, min=-most, max=most).astype(held_as)


def setup_inputs(seed: int = 0) -> dict:
    key_of = jax.random.split(jax.random.key(seed), 13)
    return {
        "strain_map": normal_values(key_of[0], (36, ELEMS), 12 ** -0.5, 1.75, ((1, 512),), jnp.float32),
        "corner_nodes": draw_corner_nodes(jax.random.fold_in(key_of[12], 71), 0),
        "counts": draw_counts(jax.random.fold_in(key_of[12], 71), 0),
        "seam_nodes": set_ends(jax.random.randint(key_of[3], (SECTORS, SEAM), 0, NODES_SEC), jax.random.fold_in(key_of[3], 1), 0, NODES_SEC - 1).astype(jnp.int32),
        "velocity": normal_values(key_of[4], (3, NODES), 1.0, 6.0, ((1, 512),), jnp.float32),
        "dual_state": normal_values(key_of[5], (3, ELEMS), 1.0, 6.0, ((1, 512),), jnp.float32),
        "nodal_load": normal_values(key_of[6], (3, NODES), 1.0, 6.0, ((1, 512),), jnp.float32),
        "mobility": jnp.clip(jnp.exp(math.log(0.5) - 1.609438 * jax.random.uniform(key_of[7], (NODES,), jnp.float32) ** shard_levels(key_of[7], (NODES,), ((0, 512),), -0.2, 0.2)), 0.1, 0.5),
        "past_dual": normal_values(key_of[8], (DEPTH, 3, ELEMS), 1.0, 6.0, ((2, 512),), jnp.float32),
        "past_dual_gap": draw_past_dual_gap(jax.random.fold_in(key_of[12], 71), 0),
        "past_velocity": normal_values(key_of[10], (DEPTH, 3, NODES), 1.0, 6.0, ((2, 512),), jnp.float32),
        "past_velocity_gap": draw_past_velocity_gap(jax.random.fold_in(key_of[12], 71), 0),
    }


def project_cone(trial):
    center = 0.5 * (trial[0] + trial[1])
    spread = 0.5 * (trial[0] - trial[1])
    shear = trial[2]
    radius = jnp.sqrt(spread * spread + shear * shear)
    upper = center + radius
    lower = center - radius
    iso_part = 0.5 * (jnp.maximum(upper, 0.0) + jnp.maximum(lower, 0.0))
    factor = jnp.clip((center + radius) / (2.0 * jnp.maximum(radius, 0.05)), 0.0, 1.0)
    return jnp.stack([iso_part + factor * spread, iso_part - factor * spread, factor * shear])

def reference(strain_map, corner_nodes, counts, seam_nodes, velocity, dual_state, nodal_load, mobility, past_dual, past_dual_gap, past_velocity, past_velocity_gap):
    highest = lax.Precision.HIGHEST
    elem_count = strain_map.shape[1]
    elem_index = jnp.arange(elem_count, dtype=jnp.int32)
    alive_mask = (elem_index % E_DEV < counts[elem_index // E_DEV]).astype(jnp.float32)
    sector_index = elem_index // ESEC
    next_sector = (sector_index + 1) % SECTORS
    seam_pos = jnp.clip(corner_nodes - NODES_SEC, 0, SEAM - 1).astype(jnp.int32)
    seam_node = seam_nodes[jnp.broadcast_to(next_sector[None, :], corner_nodes.shape), seam_pos]
    glob = jnp.where(corner_nodes < NODES_SEC, sector_index[None, :] * NODES_SEC + corner_nodes, next_sector[None, :] * NODES_SEC + seam_node).astype(jnp.int32)
    flat_nodes = glob.reshape(-1)
    strain_blocks = strain_map.reshape(3, 4, 3, elem_count)

    def sweep_once(dual, speed):
        corner_vel = speed[:, flat_nodes].reshape(3, 4, elem_count).transpose(1, 0, 2)
        rate = lax.optimization_barrier(jnp.sum(strain_blocks * corner_vel[None], axis=(1, 2)))
        trial = rate + dual
        cone = project_cone(trial)
        dual_next = alive_mask * (trial - cone)
        misfit = alive_mask * (rate - cone + dual_next)
        elem_force = lax.optimization_barrier(jnp.sum(strain_blocks * misfit[:, None, None, :], axis=0))
        spread_force = elem_force.transpose(1, 0, 2).reshape(3, -1)
        forces = jnp.zeros((3, NODES), jnp.float32).at[:, flat_nodes].add(spread_force)
        speed_next = speed - mobility[None, :] * (forces - nodal_load)
        return (dual_next, speed_next)
    dual, speed = (dual_state, velocity)
    dual_prev, speed_prev = (dual, speed)
    for sweep in range(ITERS):
        dual_prev, speed_prev = (dual, speed)
        dual, speed = sweep_once(dual, speed)
    res_w = dual - dual_prev
    res_u = speed - speed_prev
    gap_w = res_w[None] - past_dual_gap
    gap_u = res_u[None] - past_velocity_gap
    gram = jnp.einsum('iab,jab->ij', gap_w, gap_w, precision=highest) + jnp.einsum('iab,jab->ij', gap_u, gap_u, precision=highest)
    rhs = jnp.einsum('iab,ab->i', gap_w, res_w, precision=highest) + jnp.einsum('iab,ab->i', gap_u, res_u, precision=highest)
    ridge_term = 0.0001 * jnp.trace(gram) / DEPTH
    factor = jnp.linalg.cholesky(gram + ridge_term * jnp.eye(DEPTH, dtype=gram.dtype))
    coeffs = jax.scipy.linalg.cho_solve((factor, True), rhs)
    new_dual = dual - jnp.einsum('i,iab->ab', coeffs, dual[None] - past_dual - past_dual_gap, precision=highest)
    new_velocity = speed - jnp.einsum('i,iab->ab', coeffs, speed[None] - past_velocity - past_velocity_gap, precision=highest)
    return (new_velocity, new_dual)
```

```python
import functools

import jax
import jax.numpy as jnp
from jax import lax
from jax.experimental import pallas as pl
from jax.experimental.pallas import tpu as pltpu
from jax.sharding import PartitionSpec as P

MESH = pl.DeviceIdType.MESH
ITERS = 2
LANES = 128


def row_bcast(x, r):
    return jnp.broadcast_to(x[r : r + 1, :], (8, LANES))


def lane_take(row, index):
    return jnp.take_along_axis(row, index, axis=1, mode="promise_in_bounds")


def sum_corners(x, iota_row):
    odd = lax.rem(iota_row, 2) == 1
    x = x + jnp.where(odd, pltpu.roll(x, 1, 0), pltpu.roll(x, 7, 0))
    high = lax.rem(iota_row, 4) >= 2
    return x + jnp.where(high, pltpu.roll(x, 2, 0), pltpu.roll(x, 6, 0))


def project_cone(a, b, shear):
    center = 0.5 * (a + b)
    spread = 0.5 * (a - b)
    radius = jnp.sqrt(spread * spread + shear * shear)
    upper = center + radius
    lower = center - radius
    iso_part = 0.5 * (jnp.maximum(upper, 0.0) + jnp.maximum(lower, 0.0))
    factor = jnp.clip(upper / (2.0 * jnp.maximum(radius, 0.05)), 0.0, 1.0)
    return iso_part + factor * spread, iso_part - factor * spread, factor * shear


def kernel(
    sectors,
    doms,
    strain,
    corner,
    counts,
    seam,
    velocity,
    dual,
    load,
    mobility,
    past_dual,
    past_dual_gap,
    past_velocity,
    past_velocity_gap,
    new_velocity,
    new_dual,
    speed,
    load6,
    mob6,
    strain_r,
    seam_in,
    speed_in,
    edge_in,
    force,
    force_in,
    push_in,
    onehot,
    gram_out,
    gram_in,
    total_out,
    total_in,
    send_sem,
    recv_sem,
):
    sec = lax.axis_index("sector")
    dom = lax.axis_index("dom")
    prev_sec = lax.rem(sec + sectors - 1, sectors)
    next_sec = lax.rem(sec + 1, sectors)
    left = lax.rem(dom + doms - 1, doms)
    right = lax.rem(dom + 1, doms)

    def copy(src, dst, sem, s, d):
        return pltpu.make_async_remote_copy(
            src_ref=src,
            dst_ref=dst,
            send_sem=send_sem.at[sem],
            recv_sem=recv_sem.at[sem],
            device_id=(s, d),
            device_id_type=MESH,
        )

    def far_first(k):
        step = (k + 1) // 2
        return lax.rem(dom + doms // 2 + jnp.where(lax.rem(k, 2) == 1, doms - step, step), doms)

    barrier = pltpu.get_barrier_semaphore()

    def signal(s, d):
        pl.semaphore_signal(barrier, inc=1, device_id=(s, d), device_id_type=MESH)

    def greet_dom(k, c):
        d = far_first(k)
        signal(prev_sec, d)
        signal(next_sec, d)
        return c

    def greet_own(k, c):
        signal(sec, far_first(k))
        return c

    def greet_sec(o, c):
        signal(lax.rem(sec + o, sectors), dom)
        return c

    lax.fori_loop(0, doms, greet_dom, 0)
    lax.fori_loop(0, doms - 1, greet_own, 0)
    lax.fori_loop(2, sectors - 1, greet_sec, 0)

    iota_row = lax.broadcasted_iota(jnp.int32, (8, LANES), 0)
    iota_lane = lax.broadcasted_iota(jnp.int32, (8, LANES), 1)

    speed[...] = jnp.zeros_like(speed)
    load6[...] = jnp.zeros_like(load6)
    for j in range(3):
        for h in range(2):
            r, cols = 2 * j + h, pl.ds(LANES * h, LANES)
            speed[0, r : r + 1, :] = velocity[j : j + 1, cols]
            load6[r : r + 1, :] = load[j : j + 1, cols]
    mob6[...] = jnp.where(
        lax.rem(iota_row, 2) == 0,
        jnp.broadcast_to(mobility[0:1, :], (8, LANES)),
        jnp.broadcast_to(mobility[1:2, :], (8, LANES)),
    )

    pl.semaphore_wait(barrier, 2 * doms + (doms - 1) + (sectors - 3))

    six = pl.ds(0, 6)

    def send_speed(it):
        def body(k, c):
            d = far_first(k)
            copy(speed.at[it, six], speed_in.at[it, dom, six], 8 * it + 0, prev_sec, d).start()
            return c

        copy(speed.at[it, six], edge_in.at[it, 0, six], 8 * it + 1, sec, right).start()
        copy(speed.at[it, six], edge_in.at[it, 1, six], 8 * it + 2, sec, left).start()
        lax.fori_loop(0, doms, body, 0)

    def wait_speed(it):
        copy(speed.at[it, six], edge_in.at[it, 0, six], 8 * it + 1, sec, right).wait()
        copy(speed.at[it, six], edge_in.at[it, 1, six], 8 * it + 2, sec, left).wait()
        block = speed_in.at[it, :, six]
        copy(block, block, 8 * it + 0, prev_sec, dom).wait()

    def send_force(it):
        def body(k, c):
            d = far_first(k)
            copy(force.at[it, 2 + d, six], force_in.at[it, dom, six], 8 * it + 3, next_sec, d).start()
            return c

        copy(force.at[it, 0, six], push_in.at[it, 1, six], 8 * it + 4, sec, left).start()
        copy(force.at[it, 1, six], push_in.at[it, 0, six], 8 * it + 5, sec, right).start()
        lax.fori_loop(0, doms, body, 0)

    def wait_force(it):
        copy(force.at[it, 0, six], push_in.at[it, 1, six], 8 * it + 4, sec, left).wait()
        copy(force.at[it, 1, six], push_in.at[it, 0, six], 8 * it + 5, sec, right).wait()
        block = force_in.at[it, :, six]
        copy(block, block, 8 * it + 3, next_sec, dom).wait()

    seam_copy = copy(seam, seam_in, 6, prev_sec, dom)
    seam_copy.start()
    send_speed(0)

    for c in range(3):
        for j in range(3):
            for k in range(4):
                r = 12 * c + 3 * k + j
                for h in range(2):
                    strain_r[3 * c + j, 4 * h + k : 4 * h + k + 1, :] = strain[r : r + 1, pl.ds(LANES * h, LANES)]
    nodes = jnp.concatenate([corner[:, 0:LANES], corner[:, LANES : 2 * LANES]], axis=0)
    slot = LANES * (iota_row // 4) + iota_lane
    alive = jnp.where(slot < counts[0], 1.0, 0.0)
    dual_prev = [
        jnp.where(
            iota_row < 4,
            jnp.broadcast_to(dual[c : c + 1, 0:LANES], (8, LANES)),
            jnp.broadcast_to(dual[c : c + 1, LANES : 2 * LANES], (8, LANES)),
        )
        for c in range(3)
    ]

    sector_nodes = doms * 2 * LANES
    seam_copy.wait()
    position = nodes - sector_nodes
    place = jnp.bitwise_and(position, LANES - 1)
    place_row = jnp.right_shift(position, 7)
    seam_node = jnp.zeros((8, LANES), jnp.int32)
    for r in range(seam.shape[1] // LANES):
        row = jnp.broadcast_to(seam_in[0:1, LANES * r : LANES * (r + 1)], (8, LANES))
        seam_node = jnp.where(place_row == r, lane_take(row, place), seam_node)
    is_seam = position >= 0
    key = jnp.where(is_seam, 4 + jnp.right_shift(seam_node, 7), jnp.right_shift(nodes, 7) - 2 * dom + 1)
    low = jnp.bitwise_and(jnp.where(is_seam, seam_node, nodes), LANES - 1)

    lane_is = lax.broadcasted_iota(jnp.int32, (LANES, LANES), 0)
    for t in range(8):
        hit = lane_is == jnp.broadcast_to(low[t : t + 1, :], (LANES, LANES))
        onehot[:, LANES * t : LANES * (t + 1)] = jnp.where(hit, 1.0, 0.0).astype(jnp.bfloat16)

    def elements(it, dual_now):
        def look(table, row_key, acc, h):
            out = []
            for j in range(3):
                row = jnp.broadcast_to(table[2 * j + h : 2 * j + h + 1, :], (8, LANES))
                out.append(jnp.where(key == row_key, lane_take(row, low), acc[j]))
            return out

        acc = [jnp.zeros((8, LANES), jnp.float32)] * 3
        acc = look(edge_in.at[it, 0], 0, acc, 1)
        acc = look(speed.at[it], 1, acc, 0)
        acc = look(speed.at[it], 2, acc, 1)
        acc = look(edge_in.at[it, 1], 3, acc, 0)

        def body(b, acc):
            acc = look(speed_in.at[it, b], 4 + 2 * b, acc, 0)
            return tuple(look(speed_in.at[it, b], 5 + 2 * b, acc, 1))

        acc = lax.fori_loop(0, doms, body, tuple(acc))
        rate = []
        for c in range(3):
            part = strain_r[3 * c] * acc[0] + strain_r[3 * c + 1] * acc[1] + strain_r[3 * c + 2] * acc[2]
            rate.append(sum_corners(part, iota_row))
        trial = [rate[c] + dual_now[c] for c in range(3)]
        cone = project_cone(*trial)
        dual_next = [alive * (trial[c] - cone[c]) for c in range(3)]
        misfit = [alive * (rate[c] - cone[c] + dual_next[c]) for c in range(3)]
        push = [
            strain_r[j] * misfit[0] + strain_r[3 + j] * misfit[1] + strain_r[6 + j] * misfit[2] for j in range(3)
        ]
        return dual_next, push

    def spread(it, push):
        wanted, split = [], [[], [], []]
        for t in range(8):
            value = jnp.where(iota_row < 2, row_bcast(push[0], t), row_bcast(push[1], t))
            value = jnp.where(iota_row < 4, value, row_bcast(push[2], t))
            value = jnp.where(iota_row < 6, value, 0.0)
            wanted.append(row_bcast(key, t) - jnp.bitwise_and(iota_row, 1))
            for s in range(3):
                piece = value.astype(jnp.bfloat16).astype(jnp.float32)
                split[s].append(piece)
                value = value - piece
        wanted = jnp.concatenate(wanted, axis=1)
        split = [jnp.concatenate(p, axis=1) for p in split]

        def body(q, c):
            total = jnp.zeros((16, LANES), jnp.float32)
            for s in range(3):
                pair = [jnp.where(wanted == 4 * q + 2 * i, split[s], 0.0) for i in range(2)]
                left_side = jnp.concatenate(pair, axis=0).astype(jnp.bfloat16)
                total = total + lax.dot_general(
                    left_side,
                    onehot[...],
                    (((1,), (1,)), ((), ())),
                    preferred_element_type=jnp.float32,
                )
            force[it, 2 * q] = total[0:8]
            force[it, 2 * q + 1] = total[8:16]
            return c

        lax.fori_loop(0, (doms + 2) // 2, body, 0)

    def next_speed(it):
        even = lax.rem(iota_row, 2) == 0
        own = jnp.where(
            even,
            pltpu.roll(force[it, 0] + jnp.where(iota_row < 6, push_in[it, 0], 0.0), 7, 0),
            pltpu.roll(force[it, 1] + jnp.where(iota_row < 6, push_in[it, 1], 0.0), 1, 0),
        )

        def body(b, acc):
            return acc + force_in[it, b]

        own = lax.fori_loop(0, doms, body, own)
        step = speed[it] - mob6[...] * (own - load6[...])
        return jnp.where(iota_row < 6, step, 0.0)

    wait_speed(0)
    dual_one, push = elements(0, dual_prev)
    spread(0, push)
    send_force(0)
    wait_force(0)
    speed[1] = next_speed(0)
    send_speed(1)
    wait_speed(1)
    dual_two, push = elements(1, dual_one)
    spread(1, push)
    send_force(1)

    def by_history(ref, j, h):
        return ref[:, j, pl.ds(LANES * h, LANES)]

    depth = 8
    acc = [jnp.zeros((8, LANES), jnp.float32)] * (depth + 1)

    def add_gram(acc, res_row, past):
        res_b = jnp.broadcast_to(res_row, (8, LANES))
        gap = res_b - past
        acc = [acc[i] + gap * row_bcast(gap, i) for i in range(depth)] + [acc[depth] + gap * res_b]
        return acc

    for c in range(3):
        res = dual_two[c] - dual_one[c]
        for h in range(2):
            acc = add_gram(acc, res[4 * h : 4 * h + 1, :], by_history(past_dual_gap, c, h))

    wait_force(1)
    speed_one = speed[1]
    speed_two = next_speed(1)
    res = speed_two - speed_one
    for j in range(3):
        for h in range(2):
            r = 2 * j + h
            acc = add_gram(acc, res[r : r + 1, :], by_history(past_velocity_gap, j, h))
    packed = jnp.zeros((8, LANES), jnp.float32)
    for i in range(depth + 1):
        packed = jnp.where(iota_lane == i, jnp.sum(acc[i], axis=1, keepdims=True), packed)

    def fold(x):
        out = x[0:1, :]
        for l in range(1, 8):
            out = out + pltpu.roll(x[l : l + 1, :], 16 * l, 1)
        return out

    gram_out[0] = fold(packed)

    def send_gram(k, c):
        copy(gram_out.at[0], gram_in.at[k], 7, sec, far_first(k)).start()
        return c

    lax.fori_loop(0, doms - 1, send_gram, 0)
    block = gram_in.at[pl.ds(0, doms - 1)]
    copy(block, block, 7, sec, dom).wait()

    def add_in(o, acc):
        return acc + gram_in[o]

    total = lax.fori_loop(0, doms - 1, add_in, gram_out[0])
    total_out[0] = total

    def send_total(o, c):
        copy(total_out.at[0], total_in.at[o], 14, lax.rem(sec + o, sectors), dom).start()
        return c

    lax.fori_loop(1, sectors, send_total, 0)
    block = total_in.at[pl.ds(1, sectors - 1)]
    copy(block, block, 14, sec, dom).wait()

    def add_total(o, acc):
        return acc + total_in[o]

    total = lax.fori_loop(1, sectors, add_total, total)

    system = jnp.zeros((8, LANES), jnp.float32)
    for l in range(8):
        row = total if l == 0 else pltpu.roll(total, LANES - 16 * l, 1)
        system = jnp.where(iota_row == l, jnp.broadcast_to(row, (8, LANES)), system)

    diagonal = iota_row == iota_lane
    trace = jnp.sum(jnp.where(diagonal, system, 0.0), axis=1, keepdims=True)
    trace = jnp.sum(trace, axis=0, keepdims=True)
    ridge = jnp.broadcast_to(0.0001 * trace / depth, (8, LANES))
    system = jnp.where(diagonal, system + ridge, system)
    for k in range(depth):
        pivot_row = row_bcast(system, k)
        pivot_row = pivot_row / jnp.broadcast_to(pivot_row[:, k : k + 1], (8, LANES))
        column = jnp.broadcast_to(system[:, k : k + 1], (8, LANES))
        system = jnp.where(iota_row == k, pivot_row, system - column * pivot_row)
    coeffs = jnp.broadcast_to(system[:, depth : depth + 1], (8, LANES))

    def mixed(now_row, past, past_gap):
        now = jnp.broadcast_to(now_row, (8, LANES))
        return now_row - jnp.sum(coeffs * (now - past - past_gap), axis=0, keepdims=True)

    for j in range(3):
        for h in range(2):
            r, cols = 2 * j + h, pl.ds(LANES * h, LANES)
            new_velocity[j : j + 1, cols] = mixed(
                speed_two[r : r + 1, :], by_history(past_velocity, j, h), by_history(past_velocity_gap, j, h)
            )
            new_dual[j : j + 1, cols] = mixed(
                dual_two[j][4 * h : 4 * h + 1, :], by_history(past_dual, j, h), by_history(past_dual_gap, j, h)
            )


def per_device(
    strain_map,
    corner_nodes,
    counts,
    seam_nodes,
    velocity,
    dual_state,
    nodal_load,
    mobility,
    past_dual,
    past_dual_gap,
    past_velocity,
    past_velocity_gap,
):
    sectors, doms = lax.axis_size("sector"), lax.axis_size("dom")
    out = jax.ShapeDtypeStruct(velocity.shape, jnp.float32)
    vmem = pl.BlockSpec(memory_space=pltpu.VMEM)
    smem = pl.BlockSpec(memory_space=pltpu.SMEM)
    f32 = jnp.float32
    return pl.pallas_call(
        functools.partial(kernel, sectors, doms),
        out_shape=(out, out),
        in_specs=[vmem, vmem, smem] + [vmem] * 9,
        out_specs=(vmem, vmem),
        scratch_shapes=[
            pltpu.VMEM((2, 8, LANES), f32),
            pltpu.VMEM((8, LANES), f32),
            pltpu.VMEM((8, LANES), f32),
            pltpu.VMEM((9, 8, LANES), f32),
            pltpu.VMEM(seam_nodes.shape, jnp.int32),
            pltpu.VMEM((2, doms, 8, LANES), f32),
            pltpu.VMEM((2, 2, 8, LANES), f32),
            pltpu.VMEM((2, doms + 2, 8, LANES), f32),
            pltpu.VMEM((2, doms, 8, LANES), f32),
            pltpu.VMEM((2, 2, 8, LANES), f32),
            pltpu.VMEM((LANES, 8 * LANES), jnp.bfloat16),
            pltpu.VMEM((1, 1, LANES), f32),
            pltpu.VMEM((doms, 1, LANES), f32),
            pltpu.VMEM((1, 1, LANES), f32),
            pltpu.VMEM((sectors, 1, LANES), f32),
            pltpu.SemaphoreType.DMA((16,)),
            pltpu.SemaphoreType.DMA((16,)),
        ],
        compiler_params=pltpu.CompilerParams(collective_id=0, has_side_effects=True),
        name="dome",
    )(
        strain_map,
        corner_nodes,
        counts,
        seam_nodes,
        velocity,
        dual_state,
        nodal_load,
        mobility.reshape(2, LANES),
        past_dual,
        past_dual_gap,
        past_velocity,
        past_velocity_gap,
    )


def solution(mesh):
    part = ("sector", "dom")
    in_specs = (
        P(None, part),
        P(None, part),
        P(part),
        P("sector", None),
        P(None, part),
        P(None, part),
        P(None, part),
        P(part),
        P(None, None, part),
        P(None, None, part),
        P(None, None, part),
        P(None, None, part),
    )
    out_specs = (P(None, part), P(None, part))
    return jax.shard_map(per_device, mesh=mesh, in_specs=in_specs, out_specs=out_specs, check_vma=False)
```

```python
import functools

import jax
import jax.numpy as jnp
from jax import lax
from jax.experimental import pallas as pl
from jax.experimental.pallas import tpu as pltpu
from jax.sharding import PartitionSpec as P

MESH = pl.DeviceIdType.MESH
ITERS = 2
LANES = 128


def row_bcast(x, r):
    return jnp.broadcast_to(x[r : r + 1, :], (8, LANES))


def lane_take(row, index):
    return jnp.take_along_axis(row, index, axis=1, mode="promise_in_bounds")


def sum_corners(x, iota_row):
    odd = lax.rem(iota_row, 2) == 1
    x = x + jnp.where(odd, pltpu.roll(x, 1, 0), pltpu.roll(x, 7, 0))
    high = lax.rem(iota_row, 4) >= 2
    return x + jnp.where(high, pltpu.roll(x, 2, 0), pltpu.roll(x, 6, 0))


def project_cone(a, b, shear):
    center = 0.5 * (a + b)
    spread = 0.5 * (a - b)
    radius = jnp.sqrt(spread * spread + shear * shear)
    upper = center + radius
    lower = center - radius
    iso_part = 0.5 * (jnp.maximum(upper, 0.0) + jnp.maximum(lower, 0.0))
    factor = jnp.clip(upper / (2.0 * jnp.maximum(radius, 0.05)), 0.0, 1.0)
    return iso_part + factor * spread, iso_part - factor * spread, factor * shear


def kernel(
    sectors,
    doms,
    strain,
    corner,
    counts,
    seam,
    velocity,
    dual,
    load,
    mobility,
    past_dual,
    past_dual_gap,
    past_velocity,
    past_velocity_gap,
    new_velocity,
    new_dual,
    speed,
    load6,
    mob6,
    strain_r,
    seam_in,
    speed_in,
    edge_in,
    force,
    force_in,
    push_in,
    onehot,
    lhs_far,
    lhs_near,
    gram_out,
    gram_in,
    total_out,
    total_in,
    send_sem,
    recv_sem,
):
    sec = lax.axis_index("sector")
    dom = lax.axis_index("dom")
    prev_sec = lax.rem(sec + sectors - 1, sectors)
    next_sec = lax.rem(sec + 1, sectors)
    left = lax.rem(dom + doms - 1, doms)
    right = lax.rem(dom + 1, doms)

    def copy(src, dst, sem, s, d):
        return pltpu.make_async_remote_copy(
            src_ref=src,
            dst_ref=dst,
            send_sem=send_sem.at[sem],
            recv_sem=recv_sem.at[sem],
            device_id=(s, d),
            device_id_type=MESH,
        )

    def far_first(k):
        step = (k + 1) // 2
        return lax.rem(dom + doms // 2 + jnp.where(lax.rem(k, 2) == 1, doms - step, step), doms)

    barrier = pltpu.get_barrier_semaphore()

    def signal(s, d):
        pl.semaphore_signal(barrier, inc=1, device_id=(s, d), device_id_type=MESH)

    def greet_dom(k, c):
        d = far_first(k)
        signal(prev_sec, d)
        signal(next_sec, d)
        return c

    def greet_own(k, c):
        signal(sec, far_first(k))
        return c

    def greet_sec(o, c):
        signal(lax.rem(sec + o, sectors), dom)
        return c

    lax.fori_loop(0, doms, greet_dom, 0)
    lax.fori_loop(0, doms - 1, greet_own, 0)
    lax.fori_loop(2, sectors - 1, greet_sec, 0)

    iota_row = lax.broadcasted_iota(jnp.int32, (8, LANES), 0)
    iota_lane = lax.broadcasted_iota(jnp.int32, (8, LANES), 1)

    speed[...] = jnp.zeros_like(speed)
    load6[...] = jnp.zeros_like(load6)
    for j in range(3):
        for h in range(2):
            r, cols = 2 * j + h, pl.ds(LANES * h, LANES)
            speed[0, r : r + 1, :] = velocity[j : j + 1, cols]
            load6[r : r + 1, :] = load[j : j + 1, cols]
    mob6[...] = jnp.where(
        lax.rem(iota_row, 2) == 0,
        jnp.broadcast_to(mobility[0:1, :], (8, LANES)),
        jnp.broadcast_to(mobility[1:2, :], (8, LANES)),
    )

    pl.semaphore_wait(barrier, 2 * doms + (doms - 1) + (sectors - 3))

    six = pl.ds(0, 6)

    def send_speed(it):
        def body(k, c):
            d = far_first(k)
            copy(speed.at[it, six], speed_in.at[it, dom, six], 8 * it + 0, prev_sec, d).start()
            return c

        copy(speed.at[it, six], edge_in.at[it, 0, six], 8 * it + 1, sec, right).start()
        copy(speed.at[it, six], edge_in.at[it, 1, six], 8 * it + 2, sec, left).start()
        lax.fori_loop(0, doms, body, 0)

    def wait_speed(it):
        copy(speed.at[it, six], edge_in.at[it, 0, six], 8 * it + 1, sec, right).wait()
        copy(speed.at[it, six], edge_in.at[it, 1, six], 8 * it + 2, sec, left).wait()
        block = speed_in.at[it, :, six]
        copy(block, block, 8 * it + 0, prev_sec, dom).wait()

    def wait_force(it):
        copy(force.at[it, doms, six], push_in.at[it, 1, six], 8 * it + 4, sec, left).wait()
        copy(force.at[it, doms + 1, six], push_in.at[it, 0, six], 8 * it + 5, sec, right).wait()
        block = force_in.at[it, :, six]
        copy(block, block, 8 * it + 3, next_sec, dom).wait()

    seam_copy = copy(seam, seam_in, 6, prev_sec, dom)
    seam_copy.start()
    send_speed(0)

    for c in range(3):
        for j in range(3):
            for k in range(4):
                r = 12 * c + 3 * k + j
                for h in range(2):
                    strain_r[3 * c + j, 4 * h + k : 4 * h + k + 1, :] = strain[r : r + 1, pl.ds(LANES * h, LANES)]
    nodes = jnp.concatenate([corner[:, 0:LANES], corner[:, LANES : 2 * LANES]], axis=0)
    slot = LANES * (iota_row // 4) + iota_lane
    alive = jnp.where(slot < counts[0], 1.0, 0.0)
    dual_prev = [
        jnp.where(
            iota_row < 4,
            jnp.broadcast_to(dual[c : c + 1, 0:LANES], (8, LANES)),
            jnp.broadcast_to(dual[c : c + 1, LANES : 2 * LANES], (8, LANES)),
        )
        for c in range(3)
    ]

    sector_nodes = doms * 2 * LANES
    seam_copy.wait()
    position = nodes - sector_nodes
    place = jnp.bitwise_and(position, LANES - 1)
    place_row = jnp.right_shift(position, 7)
    seam_node = jnp.zeros((8, LANES), jnp.int32)
    for r in range(seam.shape[1] // LANES):
        row = jnp.broadcast_to(seam_in[0:1, LANES * r : LANES * (r + 1)], (8, LANES))
        seam_node = jnp.where(place_row == r, lane_take(row, place), seam_node)
    is_seam = position >= 0
    key = jnp.where(is_seam, 4 + jnp.right_shift(seam_node, 7), jnp.right_shift(nodes, 7) - 2 * dom + 1)
    low = jnp.bitwise_and(jnp.where(is_seam, seam_node, nodes), LANES - 1)

    lane_is = lax.broadcasted_iota(jnp.int32, (LANES, LANES), 0)
    for t in range(8):
        hit = lane_is == jnp.broadcast_to(low[t : t + 1, :], (LANES, LANES))
        onehot[:, LANES * t : LANES * (t + 1)] = jnp.where(hit, 1.0, 0.0).astype(jnp.bfloat16)

    def elements(it, dual_now):
        def look(table, row_key, acc, h):
            out = []
            for j in range(3):
                row = jnp.broadcast_to(table[2 * j + h : 2 * j + h + 1, :], (8, LANES))
                out.append(jnp.where(key == row_key, lane_take(row, low), acc[j]))
            return out

        acc = [jnp.zeros((8, LANES), jnp.float32)] * 3
        acc = look(edge_in.at[it, 0], 0, acc, 1)
        acc = look(speed.at[it], 1, acc, 0)
        acc = look(speed.at[it], 2, acc, 1)
        acc = look(edge_in.at[it, 1], 3, acc, 0)

        for b in range(doms):
            acc = look(speed_in.at[it, b], 4 + 2 * b, acc, 0)
            acc = look(speed_in.at[it, b], 5 + 2 * b, acc, 1)
        rate = []
        for c in range(3):
            part = strain_r[3 * c] * acc[0] + strain_r[3 * c + 1] * acc[1] + strain_r[3 * c + 2] * acc[2]
            rate.append(sum_corners(part, iota_row))
        trial = [rate[c] + dual_now[c] for c in range(3)]
        cone = project_cone(*trial)
        dual_next = [alive * (trial[c] - cone[c]) for c in range(3)]
        misfit = [alive * (rate[c] - cone[c] + dual_next[c]) for c in range(3)]
        push = [
            strain_r[j] * misfit[0] + strain_r[3 + j] * misfit[1] + strain_r[6 + j] * misfit[2] for j in range(3)
        ]
        return dual_next, push

    def spread(it, push):
        wanted, split = [], [[], [], []]
        for t in range(8):
            value = jnp.where(iota_row < 2, row_bcast(push[0], t), row_bcast(push[1], t))
            value = jnp.where(iota_row < 4, value, row_bcast(push[2], t))
            value = jnp.where(iota_row < 6, value, 0.0)
            wanted.append(row_bcast(key, t) - jnp.bitwise_and(iota_row, 1))
            for s in range(3):
                piece = value.astype(jnp.bfloat16).astype(jnp.float32)
                split[s].append(piece)
                value = value - piece
        wanted = jnp.concatenate(wanted, axis=1)
        split = [jnp.concatenate(p, axis=1) for p in split]

        def fill(lhs, q, keys):
            hits = [wanted == k for k in keys]
            for s in range(3):
                pair = jnp.concatenate([jnp.where(hit, split[s], 0.0) for hit in hits], axis=0)
                lhs[s, pl.ds(pl.multiple_of(16 * q, 16), 16), :] = pair.astype(jnp.bfloat16)

        def product(lhs):
            rows = lhs.shape[1]
            out = lax.dot_general(
                lhs[...].reshape(3 * rows, 8 * LANES),
                onehot[...],
                (((1,), (1,)), ((), ())),
                preferred_element_type=jnp.float32,
            ).reshape(3, rows // 8, 8, LANES)
            return (out[2] + out[1]) + out[0]

        def fill_far(q, c):
            fill(lhs_far, q, [4 + 2 * far_first(2 * q + i) for i in range(2)])
            return c

        def fill_near(q, c):
            fill(lhs_near, q, [4 + 2 * far_first(half + 2 * q + i) for i in range(2)])
            return c

        def send(k, c):
            copy(force.at[it, k, six], force_in.at[it, dom, six], 8 * it + 3, next_sec, far_first(k)).start()
            return c

        half = doms // 2
        lax.fori_loop(0, half // 2, fill_far, 0)
        force[it, 0:half] = product(lhs_far)
        lax.fori_loop(0, half, send, 0)
        lax.fori_loop(0, half // 2, fill_near, 0)
        fill(lhs_near, half // 2, [0, 2])
        force[it, half : doms + 2] = product(lhs_near)
        lax.fori_loop(half, doms, send, 0)
        copy(force.at[it, doms, six], push_in.at[it, 1, six], 8 * it + 4, sec, left).start()
        copy(force.at[it, doms + 1, six], push_in.at[it, 0, six], 8 * it + 5, sec, right).start()

    def next_speed(it):
        even = lax.rem(iota_row, 2) == 0
        own = jnp.where(
            even,
            pltpu.roll(force[it, doms] + jnp.where(iota_row < 6, push_in[it, 0], 0.0), 7, 0),
            pltpu.roll(force[it, doms + 1] + jnp.where(iota_row < 6, push_in[it, 1], 0.0), 1, 0),
        )

        def body(b, acc):
            return acc + force_in[it, b]

        own = lax.fori_loop(0, doms, body, own)
        step = speed[it] - mob6[...] * (own - load6[...])
        return jnp.where(iota_row < 6, step, 0.0)

    wait_speed(0)
    dual_one, push = elements(0, dual_prev)
    spread(0, push)
    wait_force(0)
    speed[1] = next_speed(0)
    send_speed(1)
    wait_speed(1)
    dual_two, push = elements(1, dual_one)
    spread(1, push)

    def by_history(ref, j, h):
        return ref[j, :, pl.ds(LANES * h, LANES)]

    depth = 8
    acc = [jnp.zeros((8, LANES), jnp.float32)] * (depth + 1)

    def add_gram(acc, res_row, past):
        res_b = jnp.broadcast_to(res_row, (8, LANES))
        gap = res_b - past
        acc = [acc[i] + gap * row_bcast(gap, i) for i in range(depth)] + [acc[depth] + gap * res_b]
        return acc

    for c in range(3):
        res = dual_two[c] - dual_one[c]
        for h in range(2):
            acc = add_gram(acc, res[4 * h : 4 * h + 1, :], by_history(past_dual_gap, c, h))

    wait_force(1)
    speed_one = speed[1]
    speed_two = next_speed(1)
    res = speed_two - speed_one
    for j in range(3):
        for h in range(2):
            r = 2 * j + h
            acc = add_gram(acc, res[r : r + 1, :], by_history(past_velocity_gap, j, h))
    packed = jnp.zeros((8, LANES), jnp.float32)
    for i in range(depth + 1):
        packed = jnp.where(iota_lane == i, jnp.sum(acc[i], axis=1, keepdims=True), packed)

    def fold(x):
        out = x[0:1, :]
        for l in range(1, 8):
            out = out + pltpu.roll(x[l : l + 1, :], 16 * l, 1)
        return out

    gram_out[0] = fold(packed)

    def send_gram(k, c):
        copy(gram_out.at[0], gram_in.at[k], 7, sec, far_first(k)).start()
        return c

    lax.fori_loop(0, doms - 1, send_gram, 0)
    block = gram_in.at[pl.ds(0, doms - 1)]
    copy(block, block, 7, sec, dom).wait()

    def add_in(o, acc):
        return acc + gram_in[o]

    total = lax.fori_loop(0, doms - 1, add_in, gram_out[0])
    total_out[0] = total

    def send_total(o, c):
        copy(total_out.at[0], total_in.at[o], 14, lax.rem(sec + o, sectors), dom).start()
        return c

    lax.fori_loop(1, sectors, send_total, 0)
    block = total_in.at[pl.ds(1, sectors - 1)]
    copy(block, block, 14, sec, dom).wait()

    def add_total(o, acc):
        return acc + total_in[o]

    total = lax.fori_loop(1, sectors, add_total, total)

    system = jnp.zeros((8, LANES), jnp.float32)
    for l in range(8):
        row = total if l == 0 else pltpu.roll(total, LANES - 16 * l, 1)
        system = jnp.where(iota_row == l, jnp.broadcast_to(row, (8, LANES)), system)

    diagonal = iota_row == iota_lane
    trace = jnp.sum(jnp.where(diagonal, system, 0.0), axis=1, keepdims=True)
    trace = jnp.sum(trace, axis=0, keepdims=True)
    ridge = jnp.broadcast_to(0.0001 * trace / depth, (8, LANES))
    system = jnp.where(diagonal, system + ridge, system)
    for k in range(depth):
        pivot_row = row_bcast(system, k)
        pivot_row = pivot_row / jnp.broadcast_to(pivot_row[:, k : k + 1], (8, LANES))
        column = jnp.broadcast_to(system[:, k : k + 1], (8, LANES))
        system = jnp.where(iota_row == k, pivot_row, system - column * pivot_row)
    coeffs = jnp.broadcast_to(system[:, depth : depth + 1], (8, LANES))

    def mixed(now_row, past, past_gap):
        now = jnp.broadcast_to(now_row, (8, LANES))
        return now_row - jnp.sum(coeffs * (now - past - past_gap), axis=0, keepdims=True)

    for j in range(3):
        for h in range(2):
            r, cols = 2 * j + h, pl.ds(LANES * h, LANES)
            new_velocity[j : j + 1, cols] = mixed(
                speed_two[r : r + 1, :], by_history(past_velocity, j, h), by_history(past_velocity_gap, j, h)
            )
            new_dual[j : j + 1, cols] = mixed(
                dual_two[j][4 * h : 4 * h + 1, :], by_history(past_dual, j, h), by_history(past_dual_gap, j, h)
            )


def per_device(
    strain_map,
    corner_nodes,
    counts,
    seam_nodes,
    velocity,
    dual_state,
    nodal_load,
    mobility,
    past_dual,
    past_dual_gap,
    past_velocity,
    past_velocity_gap,
):
    sectors, doms = lax.axis_size("sector"), lax.axis_size("dom")
    out = jax.ShapeDtypeStruct(velocity.shape, jnp.float32)
    vmem = pl.BlockSpec(memory_space=pltpu.VMEM)
    smem = pl.BlockSpec(memory_space=pltpu.SMEM)
    f32 = jnp.float32
    return pl.pallas_call(
        functools.partial(kernel, sectors, doms),
        out_shape=(out, out),
        in_specs=[vmem, vmem, smem] + [vmem] * 9,
        out_specs=(vmem, vmem),
        scratch_shapes=[
            pltpu.VMEM((2, 8, LANES), f32),
            pltpu.VMEM((8, LANES), f32),
            pltpu.VMEM((8, LANES), f32),
            pltpu.VMEM((9, 8, LANES), f32),
            pltpu.VMEM(seam_nodes.shape, jnp.int32),
            pltpu.VMEM((2, doms, 8, LANES), f32),
            pltpu.VMEM((2, 2, 8, LANES), f32),
            pltpu.VMEM((2, doms + 2, 8, LANES), f32),
            pltpu.VMEM((2, doms, 8, LANES), f32),
            pltpu.VMEM((2, 2, 8, LANES), f32),
            pltpu.VMEM((LANES, 8 * LANES), jnp.bfloat16),
            pltpu.VMEM((3, 4 * doms, 8 * LANES), jnp.bfloat16),
            pltpu.VMEM((3, 4 * doms + 16, 8 * LANES), jnp.bfloat16),
            pltpu.VMEM((1, 1, LANES), f32),
            pltpu.VMEM((doms, 1, LANES), f32),
            pltpu.VMEM((1, 1, LANES), f32),
            pltpu.VMEM((sectors, 1, LANES), f32),
            pltpu.SemaphoreType.DMA((16,)),
            pltpu.SemaphoreType.DMA((16,)),
        ],
        compiler_params=pltpu.CompilerParams(collective_id=0, has_side_effects=True),
        name="dome",
    )(
        strain_map,
        corner_nodes,
        counts,
        seam_nodes,
        velocity,
        dual_state,
        nodal_load,
        mobility.reshape(2, LANES),
        past_dual.transpose(1, 0, 2),
        past_dual_gap.transpose(1, 0, 2),
        past_velocity.transpose(1, 0, 2),
        past_velocity_gap.transpose(1, 0, 2),
    )


def solution(mesh):
    part = ("sector", "dom")
    in_specs = (
        P(None, part),
        P(None, part),
        P(part),
        P("sector", None),
        P(None, part),
        P(None, part),
        P(None, part),
        P(part),
        P(None, None, part),
        P(None, None, part),
        P(None, None, part),
        P(None, None, part),
    )
    out_specs = (P(None, part), P(None, part))
    return jax.shard_map(per_device, mesh=mesh, in_specs=in_specs, out_specs=out_specs, check_vma=False)
```

```python
import functools

import jax
import jax.numpy as jnp
from jax import lax
from jax.experimental import pallas as pl
from jax.experimental.pallas import tpu as pltpu
from jax.sharding import PartitionSpec as P

MESH = pl.DeviceIdType.MESH
ITERS = 2
LANES = 128


def row_bcast(x, r):
    return jnp.broadcast_to(x[r : r + 1, :], (8, LANES))


def lane_take(row, index):
    return jnp.take_along_axis(row, index, axis=1, mode="promise_in_bounds")


def sum_corners(x, iota_row):
    odd = lax.rem(iota_row, 2) == 1
    x = x + jnp.where(odd, pltpu.roll(x, 1, 0), pltpu.roll(x, 7, 0))
    high = lax.rem(iota_row, 4) >= 2
    return x + jnp.where(high, pltpu.roll(x, 2, 0), pltpu.roll(x, 6, 0))


def project_cone(a, b, shear):
    center = 0.5 * (a + b)
    spread = 0.5 * (a - b)
    radius = jnp.sqrt(spread * spread + shear * shear)
    upper = center + radius
    lower = center - radius
    iso_part = 0.5 * (jnp.maximum(upper, 0.0) + jnp.maximum(lower, 0.0))
    factor = jnp.clip(upper / (2.0 * jnp.maximum(radius, 0.05)), 0.0, 1.0)
    return iso_part + factor * spread, iso_part - factor * spread, factor * shear


def kernel(
    sectors,
    doms,
    strain_hbm,
    corner_hbm,
    counts,
    seam_hbm,
    velocity_hbm,
    dual_hbm,
    load_hbm,
    mobility_hbm,
    past_dual_hbm,
    past_dual_gap_hbm,
    past_velocity_hbm,
    past_velocity_gap_hbm,
    result,
    strain,
    corner,
    velocity,
    dual,
    load,
    mobility,
    past_dual,
    past_dual_gap,
    past_velocity,
    past_velocity_gap,
    speed,
    load6,
    mob6,
    strain_r,
    seam_in,
    speed_in,
    edge_in,
    force,
    force_in,
    push_in,
    onehot,
    lhs_far,
    lhs_near,
    gram_out,
    gram_in,
    total_out,
    total_in,
    mask_far,
    mask_near,
    load_sem,
    send_sem,
    recv_sem,
):
    sec = lax.axis_index("sector")
    dom = lax.axis_index("dom")
    prev_sec = lax.rem(sec + sectors - 1, sectors)
    next_sec = lax.rem(sec + 1, sectors)
    left = lax.rem(dom + doms - 1, doms)
    right = lax.rem(dom + 1, doms)

    def copy(src, dst, sem, s, d):
        return pltpu.make_async_remote_copy(
            src_ref=src,
            dst_ref=dst,
            send_sem=send_sem.at[sem],
            recv_sem=recv_sem.at[sem],
            device_id=(s, d),
            device_id_type=MESH,
        )

    def far_first(k):
        step = (k + 1) // 2
        return lax.rem(dom + doms // 2 + jnp.where(lax.rem(k, 2) == 1, doms - step, step), doms)

    barrier = pltpu.get_barrier_semaphore()

    def signal(s, d):
        pl.semaphore_signal(barrier, inc=1, device_id=(s, d), device_id_type=MESH)

    def greet_dom(k, c):
        d = far_first(k)
        signal(prev_sec, d)
        signal(next_sec, d)
        return c

    def greet_own(k, c):
        signal(sec, far_first(k))
        return c

    def greet_sec(o, c):
        signal(lax.rem(sec + o, sectors), dom)
        return c

    loads = [
        pltpu.make_async_copy(src, dst, load_sem.at[i])
        for i, (src, dst) in enumerate(
            [
                (velocity_hbm, velocity),
                (load_hbm, load),
                (mobility_hbm, mobility),
                (corner_hbm, corner),
                (strain_hbm, strain),
                (dual_hbm, dual),
                (past_dual_gap_hbm, past_dual_gap),
                (past_velocity_gap_hbm, past_velocity_gap),
                (past_dual_hbm, past_dual),
                (past_velocity_hbm, past_velocity),
            ]
        )
    ]
    loads[0].start()
    lax.fori_loop(0, doms, greet_dom, 0)
    for l in loads[1:]:
        l.start()
    lax.fori_loop(0, doms - 1, greet_own, 0)
    lax.fori_loop(2, sectors - 1, greet_sec, 0)

    iota_row = lax.broadcasted_iota(jnp.int32, (8, LANES), 0)
    iota_lane = lax.broadcasted_iota(jnp.int32, (8, LANES), 1)

    speed[...] = jnp.zeros_like(speed)
    load6[...] = jnp.zeros_like(load6)
    for l in loads[0:3]:
        l.wait()
    for j in range(3):
        for h in range(2):
            r, cols = 2 * j + h, pl.ds(LANES * h, LANES)
            speed[0, r : r + 1, :] = velocity[j : j + 1, cols]
            load6[r : r + 1, :] = load[j : j + 1, cols]
    mob6[...] = jnp.where(
        lax.rem(iota_row, 2) == 0,
        jnp.broadcast_to(mobility[0:1, :], (8, LANES)),
        jnp.broadcast_to(mobility[1:2, :], (8, LANES)),
    )

    pl.semaphore_wait(barrier, 2 * doms + (doms - 1) + (sectors - 3))

    six = pl.ds(0, 6)

    def send_speed(it):
        def body(k, c):
            d = far_first(k)
            copy(speed.at[it, six], speed_in.at[it, dom, six], 8 * it + 0, prev_sec, d).start()
            return c

        copy(speed.at[it, six], edge_in.at[it, 0, six], 8 * it + 1, sec, right).start()
        copy(speed.at[it, six], edge_in.at[it, 1, six], 8 * it + 2, sec, left).start()
        lax.fori_loop(0, doms, body, 0)

    def wait_speed(it, what="wait_recv"):
        getattr(copy(speed.at[it, six], edge_in.at[it, 0, six], 8 * it + 1, sec, right), what)()
        getattr(copy(speed.at[it, six], edge_in.at[it, 1, six], 8 * it + 2, sec, left), what)()
        block = speed_in.at[it, :, six]
        getattr(copy(block, block, 8 * it + 0, prev_sec, dom), what)()

    def wait_force(it, what="wait_recv"):
        getattr(copy(force.at[it, doms, six], push_in.at[it, 1, six], 8 * it + 4, sec, left), what)()
        getattr(copy(force.at[it, doms + 1, six], push_in.at[it, 0, six], 8 * it + 5, sec, right), what)()
        block = force_in.at[it, :, six]
        getattr(copy(block, block, 8 * it + 3, next_sec, dom), what)()

    seam_copy = copy(seam_hbm, seam_in, 6, prev_sec, dom)
    seam_copy.start()
    send_speed(0)

    for l in loads[3:]:
        l.wait()
    for c in range(3):
        for j in range(3):
            for k in range(4):
                r = 12 * c + 3 * k + j
                for h in range(2):
                    strain_r[3 * c + j, 4 * h + k : 4 * h + k + 1, :] = strain[r : r + 1, pl.ds(LANES * h, LANES)]
    nodes = jnp.concatenate([corner[:, 0:LANES], corner[:, LANES : 2 * LANES]], axis=0)
    slot = LANES * (iota_row // 4) + iota_lane
    alive = jnp.where(slot < counts[0], 1.0, 0.0)
    dual_prev = [
        jnp.where(
            iota_row < 4,
            jnp.broadcast_to(dual[c : c + 1, 0:LANES], (8, LANES)),
            jnp.broadcast_to(dual[c : c + 1, LANES : 2 * LANES], (8, LANES)),
        )
        for c in range(3)
    ]

    sector_nodes = doms * 2 * LANES
    seam_copy.wait_recv()
    position = nodes - sector_nodes
    place = jnp.bitwise_and(position, LANES - 1)
    place_row = jnp.right_shift(position, 7)
    seam_node = jnp.zeros((8, LANES), jnp.int32)
    for r in range(seam_in.shape[1] // LANES):
        row = jnp.broadcast_to(seam_in[0:1, LANES * r : LANES * (r + 1)], (8, LANES))
        seam_node = jnp.where(place_row == r, lane_take(row, place), seam_node)
    is_seam = position >= 0
    key = jnp.where(is_seam, 4 + jnp.right_shift(seam_node, 7), jnp.right_shift(nodes, 7) - 2 * dom + 1)
    low = jnp.bitwise_and(jnp.where(is_seam, seam_node, nodes), LANES - 1)

    lane_is = lax.broadcasted_iota(jnp.int32, (LANES, LANES), 0)
    for t in range(8):
        hit = lane_is == jnp.broadcast_to(low[t : t + 1, :], (LANES, LANES))
        onehot[:, LANES * t : LANES * (t + 1)] = jnp.where(hit, 1.0, 0.0).astype(jnp.bfloat16)

    half = doms // 2
    wanted = jnp.concatenate([row_bcast(key, t) - jnp.bitwise_and(iota_row, 1) for t in range(8)], axis=1)

    def mark(mask, q, keys):
        pair = jnp.concatenate([jnp.where(wanted == k, 1.0, 0.0) for k in keys], axis=0)
        mask[pl.ds(pl.multiple_of(16 * q, 16), 16), :] = pair.astype(jnp.bfloat16)

    def mark_far(q, c):
        mark(mask_far, q, [4 + 2 * far_first(2 * q + i) for i in range(2)])
        return c

    def mark_near(q, c):
        mark(mask_near, q, [4 + 2 * far_first(half + 2 * q + i) for i in range(2)])
        return c

    lax.fori_loop(0, half // 2, mark_far, 0)
    lax.fori_loop(0, half // 2, mark_near, 0)
    mark(mask_near, half // 2, [0, 2])

    def elements(it, dual_now):
        def look(table, row_key, acc, h):
            out = []
            for j in range(3):
                row = jnp.broadcast_to(table[2 * j + h : 2 * j + h + 1, :], (8, LANES))
                out.append(jnp.where(key == row_key, lane_take(row, low), acc[j]))
            return out

        acc = [jnp.zeros((8, LANES), jnp.float32)] * 3
        acc = look(edge_in.at[it, 0], 0, acc, 1)
        acc = look(speed.at[it], 1, acc, 0)
        acc = look(speed.at[it], 2, acc, 1)
        acc = look(edge_in.at[it, 1], 3, acc, 0)

        for b in range(doms):
            acc = look(speed_in.at[it, b], 4 + 2 * b, acc, 0)
            acc = look(speed_in.at[it, b], 5 + 2 * b, acc, 1)
        rate = []
        for c in range(3):
            part = strain_r[3 * c] * acc[0] + strain_r[3 * c + 1] * acc[1] + strain_r[3 * c + 2] * acc[2]
            rate.append(sum_corners(part, iota_row))
        trial = [rate[c] + dual_now[c] for c in range(3)]
        cone = project_cone(*trial)
        dual_next = [alive * (trial[c] - cone[c]) for c in range(3)]
        misfit = [alive * (rate[c] - cone[c] + dual_next[c]) for c in range(3)]
        push = [
            strain_r[j] * misfit[0] + strain_r[3 + j] * misfit[1] + strain_r[6 + j] * misfit[2] for j in range(3)
        ]
        return dual_next, push

    def spread(it, push):
        split = [[], [], []]
        for t in range(8):
            value = jnp.where(iota_row < 2, row_bcast(push[0], t), row_bcast(push[1], t))
            value = jnp.where(iota_row < 4, value, row_bcast(push[2], t))
            value = jnp.where(iota_row < 6, value, 0.0)
            for s in range(3):
                piece = value.astype(jnp.bfloat16).astype(jnp.float32)
                split[s].append(piece)
                value = value - piece
        split = [jnp.concatenate(p, axis=1) for p in split]
        split = [jnp.concatenate([p, p], axis=0).astype(jnp.bfloat16) for p in split]

        def fill(lhs, mask):
            for q in range(mask.shape[0] // 16):
                rows = slice(16 * q, 16 * q + 16)
                hit = mask[rows, :]
                for s in range(3):
                    lhs[s, rows, :] = hit * split[s]

        def product(lhs):
            rows = lhs.shape[1]
            out = lax.dot_general(
                lhs[...].reshape(3 * rows, 8 * LANES),
                onehot[...],
                (((1,), (1,)), ((), ())),
                preferred_element_type=jnp.float32,
            ).reshape(3, rows // 8, 8, LANES)
            return (out[2] + out[1]) + out[0]

        def send(k, c):
            copy(force.at[it, k, six], force_in.at[it, dom, six], 8 * it + 3, next_sec, far_first(k)).start()
            return c

        fill(lhs_far, mask_far)
        force[it, 0:half] = product(lhs_far)
        lax.fori_loop(0, half, send, 0)
        fill(lhs_near, mask_near)
        force[it, half : doms + 2] = product(lhs_near)
        lax.fori_loop(half, doms, send, 0)
        copy(force.at[it, doms, six], push_in.at[it, 1, six], 8 * it + 4, sec, left).start()
        copy(force.at[it, doms + 1, six], push_in.at[it, 0, six], 8 * it + 5, sec, right).start()

    def next_speed(it):
        even = lax.rem(iota_row, 2) == 0
        own = jnp.where(
            even,
            pltpu.roll(force[it, doms] + jnp.where(iota_row < 6, push_in[it, 0], 0.0), 7, 0),
            pltpu.roll(force[it, doms + 1] + jnp.where(iota_row < 6, push_in[it, 1], 0.0), 1, 0),
        )

        def body(b, acc):
            return acc + force_in[it, b]

        own = lax.fori_loop(0, doms, body, own)
        step = speed[it] - mob6[...] * (own - load6[...])
        return jnp.where(iota_row < 6, step, 0.0)

    wait_speed(0)
    dual_one, push = elements(0, dual_prev)
    spread(0, push)
    wait_force(0)
    speed[1] = next_speed(0)
    send_speed(1)
    wait_speed(1)
    dual_two, push = elements(1, dual_one)
    spread(1, push)

    def by_history(ref, j, h):
        return ref[j, :, pl.ds(LANES * h, LANES)]

    depth = 8
    acc = [jnp.zeros((8, LANES), jnp.float32)] * (depth + 1)

    def add_gram(acc, res_row, past):
        res_b = jnp.broadcast_to(res_row, (8, LANES))
        gap = res_b - past
        acc = [acc[i] + gap * row_bcast(gap, i) for i in range(depth)] + [acc[depth] + gap * res_b]
        return acc

    for c in range(3):
        res = dual_two[c] - dual_one[c]
        for h in range(2):
            acc = add_gram(acc, res[4 * h : 4 * h + 1, :], by_history(past_dual_gap, c, h))

    wait_force(1)
    speed_one = speed[1]
    speed_two = next_speed(1)
    res = speed_two - speed_one
    for j in range(3):
        for h in range(2):
            r = 2 * j + h
            acc = add_gram(acc, res[r : r + 1, :], by_history(past_velocity_gap, j, h))
    packed = jnp.zeros((8, LANES), jnp.float32)
    for i in range(depth + 1):
        packed = jnp.where(iota_lane == i, jnp.sum(acc[i], axis=1, keepdims=True), packed)

    def fold(x):
        out = x[0:1, :]
        for l in range(1, 8):
            out = out + pltpu.roll(x[l : l + 1, :], 16 * l, 1)
        return out

    gram_out[0] = fold(packed)

    def send_gram(k, c):
        copy(gram_out.at[0], gram_in.at[k], 7, sec, far_first(k)).start()
        return c

    lax.fori_loop(0, doms - 1, send_gram, 0)
    block = gram_in.at[pl.ds(0, doms - 1)]
    gram_copies = copy(block, block, 7, sec, dom)
    gram_copies.wait_recv()

    def add_in(o, acc):
        return acc + gram_in[o]

    total = lax.fori_loop(0, doms - 1, add_in, gram_out[0])
    total_out[0] = total

    def send_total(o, c):
        copy(total_out.at[0], total_in.at[o], 14, lax.rem(sec + o, sectors), dom).start()
        return c

    lax.fori_loop(1, sectors, send_total, 0)
    block = total_in.at[pl.ds(1, sectors - 1)]
    total_copies = copy(block, block, 14, sec, dom)

    def apart(now_row, past, past_gap):
        return jnp.broadcast_to(now_row, (8, LANES)) - past - past_gap

    parts = [(j, h) for j in range(3) for h in range(2)]
    apart_u = [
        apart(speed_two[2 * j + h : 2 * j + h + 1, :], by_history(past_velocity, j, h), by_history(past_velocity_gap, j, h))
        for j, h in parts
    ]
    apart_w = [
        apart(dual_two[j][4 * h : 4 * h + 1, :], by_history(past_dual, j, h), by_history(past_dual_gap, j, h))
        for j, h in parts
    ]
    seam_copy.wait_send()
    for it in range(ITERS):
        wait_speed(it, "wait_send")
        wait_force(it, "wait_send")
    gram_copies.wait_send()
    total_copies.wait_recv()

    def add_total(o, acc):
        return acc + total_in[o]

    total = lax.fori_loop(1, sectors, add_total, total)

    def entry(lane):
        return jnp.broadcast_to(jnp.broadcast_to(total[:, lane : lane + 1], (1, LANES)), (8, LANES))

    upper = [[entry(16 * i + l) if l >= i else None for l in range(depth + 1)] for i in range(depth)]
    trace = upper[0][0]
    for i in range(1, depth):
        trace = trace + upper[i][i]
    ridge = 0.0001 * trace / depth
    for i in range(depth):
        upper[i][i] = upper[i][i] + ridge
    inverse = []
    for k in range(depth):
        inverse.append(1.0 / upper[k][k])
        for i in range(k + 1, depth):
            scale = upper[k][i] * inverse[k]
            for l in range(i, depth + 1):
                upper[i][l] = upper[i][l] - scale * upper[k][l]
    solved = [None] * depth
    for k in reversed(range(depth)):
        value = upper[k][depth]
        for l in range(k + 1, depth):
            value = value - upper[k][l] * solved[l]
        solved[k] = value * inverse[k]
    coeffs = solved[0]
    for i in range(1, depth):
        coeffs = jnp.where(iota_row == i, solved[i], coeffs)

    for p, (j, h) in enumerate(parts):
        cols = pl.ds(LANES * h, LANES)
        result[j : j + 1, cols] = speed_two[2 * j + h : 2 * j + h + 1, :] - jnp.sum(
            coeffs * apart_u[p], axis=0, keepdims=True
        )
        result[4 + j : 5 + j, cols] = dual_two[j][4 * h : 4 * h + 1, :] - jnp.sum(
            coeffs * apart_w[p], axis=0, keepdims=True
        )
    total_copies.wait_send()


def per_device(
    strain_map,
    corner_nodes,
    counts,
    seam_nodes,
    velocity,
    dual_state,
    nodal_load,
    mobility,
    past_dual,
    past_dual_gap,
    past_velocity,
    past_velocity_gap,
):
    sectors, doms = lax.axis_size("sector"), lax.axis_size("dom")
    out = jax.ShapeDtypeStruct(velocity.shape, jnp.float32)
    vmem = pl.BlockSpec(memory_space=pltpu.VMEM)
    smem = pl.BlockSpec(memory_space=pltpu.SMEM)
    hbm = pl.BlockSpec(memory_space=pl.ANY)
    history = pltpu.VMEM((3, 8, 2 * LANES), jnp.float32)
    f32 = jnp.float32
    result = pl.pallas_call(
        functools.partial(kernel, sectors, doms),
        out_shape=pltpu.VMEM((8, 2 * LANES), f32),
        in_specs=[hbm, hbm, smem] + [hbm] * 9,
        out_specs=vmem,
        scratch_shapes=[
            pltpu.VMEM(strain_map.shape, f32),
            pltpu.VMEM(corner_nodes.shape, jnp.int32),
            pltpu.VMEM(velocity.shape, f32),
            pltpu.VMEM(dual_state.shape, f32),
            pltpu.VMEM(nodal_load.shape, f32),
            pltpu.VMEM((2, LANES), f32),
            history,
            history,
            history,
            history,
            pltpu.VMEM((2, 8, LANES), f32),
            pltpu.VMEM((8, LANES), f32),
            pltpu.VMEM((8, LANES), f32),
            pltpu.VMEM((9, 8, LANES), f32),
            pltpu.VMEM(seam_nodes.shape, jnp.int32),
            pltpu.VMEM((2, doms, 8, LANES), f32),
            pltpu.VMEM((2, 2, 8, LANES), f32),
            pltpu.VMEM((2, doms + 2, 8, LANES), f32),
            pltpu.VMEM((2, doms, 8, LANES), f32),
            pltpu.VMEM((2, 2, 8, LANES), f32),
            pltpu.VMEM((LANES, 8 * LANES), jnp.bfloat16),
            pltpu.VMEM((3, 4 * doms, 8 * LANES), jnp.bfloat16),
            pltpu.VMEM((3, 4 * doms + 16, 8 * LANES), jnp.bfloat16),
            pltpu.VMEM((1, 1, LANES), f32),
            pltpu.VMEM((doms, 1, LANES), f32),
            pltpu.VMEM((1, 1, LANES), f32),
            pltpu.VMEM((sectors, 1, LANES), f32),
            pltpu.VMEM((4 * doms, 8 * LANES), jnp.bfloat16),
            pltpu.VMEM((4 * doms + 16, 8 * LANES), jnp.bfloat16),
            pltpu.SemaphoreType.DMA((10,)),
            pltpu.SemaphoreType.DMA((16,)),
            pltpu.SemaphoreType.DMA((16,)),
        ],
        compiler_params=pltpu.CompilerParams(collective_id=0, has_side_effects=True),
        name="dome",
    )(
        strain_map,
        corner_nodes,
        counts,
        seam_nodes,
        velocity,
        dual_state,
        nodal_load,
        mobility.reshape(2, LANES),
        past_dual.transpose(1, 0, 2),
        past_dual_gap.transpose(1, 0, 2),
        past_velocity.transpose(1, 0, 2),
        past_velocity_gap.transpose(1, 0, 2),
    )
    return result[0:3], result[4:7]


def solution(mesh):
    part = ("sector", "dom")
    in_specs = (
        P(None, part),
        P(None, part),
        P(part),
        P("sector", None),
        P(None, part),
        P(None, part),
        P(None, part),
        P(part),
        P(None, None, part),
        P(None, None, part),
        P(None, None, part),
        P(None, None, part),
    )
    out_specs = (P(None, part), P(None, part))
    return jax.shard_map(per_device, mesh=mesh, in_specs=in_specs, out_specs=out_specs, check_vma=False)
```

```python
import functools

import jax
import jax.numpy as jnp
from jax import lax
from jax.experimental import pallas as pl
from jax.experimental.pallas import tpu as pltpu
from jax.sharding import PartitionSpec as P

MESH = pl.DeviceIdType.MESH
ITERS = 2
LANES = 128


def row_bcast(x, r):
    return jnp.broadcast_to(x[r : r + 1, :], (8, LANES))


def lane_take(row, index):
    return jnp.take_along_axis(row, index, axis=1, mode="promise_in_bounds")


def sum_corners(x, iota_row):
    odd = lax.rem(iota_row, 2) == 1
    x = x + jnp.where(odd, pltpu.roll(x, 1, 0), pltpu.roll(x, 7, 0))
    high = lax.rem(iota_row, 4) >= 2
    return x + jnp.where(high, pltpu.roll(x, 2, 0), pltpu.roll(x, 6, 0))


def project_cone(a, b, shear):
    center = 0.5 * (a + b)
    spread = 0.5 * (a - b)
    radius = jnp.sqrt(spread * spread + shear * shear)
    upper = center + radius
    lower = center - radius
    iso_part = 0.5 * (jnp.maximum(upper, 0.0) + jnp.maximum(lower, 0.0))
    factor = jnp.clip(upper / (2.0 * jnp.maximum(radius, 0.05)), 0.0, 1.0)
    return iso_part + factor * spread, iso_part - factor * spread, factor * shear


def kernel(
    sectors,
    doms,
    strain_hbm,
    corner_hbm,
    counts,
    seam_hbm,
    velocity_hbm,
    dual_hbm,
    load_hbm,
    mobility_hbm,
    past_dual_hbm,
    past_dual_gap_hbm,
    past_velocity_hbm,
    past_velocity_gap_hbm,
    result,
    strain,
    corner,
    velocity,
    dual,
    load,
    mobility,
    past_dual,
    past_dual_gap,
    past_velocity,
    past_velocity_gap,
    speed,
    load6,
    mob6,
    strain_r,
    seam_in,
    speed_in,
    edge_in,
    force,
    force_in,
    push_in,
    onehot,
    lhs_far,
    lhs_near,
    gram_out,
    gram_in,
    total_out,
    total_in,
    mask_far,
    mask_near,
    load_sem,
    send_sem,
    recv_sem,
):
    sec = lax.axis_index("sector")
    dom = lax.axis_index("dom")
    prev_sec = lax.rem(sec + sectors - 1, sectors)
    next_sec = lax.rem(sec + 1, sectors)
    left = lax.rem(dom + doms - 1, doms)
    right = lax.rem(dom + 1, doms)

    def copy(src, dst, sem, s, d):
        return pltpu.make_async_remote_copy(
            src_ref=src,
            dst_ref=dst,
            send_sem=send_sem.at[sem],
            recv_sem=recv_sem.at[sem],
            device_id=(s, d),
            device_id_type=MESH,
        )

    def far_first(k):
        step = (k + 1) // 2
        return lax.rem(dom + doms // 2 + jnp.where(lax.rem(k, 2) == 1, doms - step, step), doms)

    barrier = pltpu.get_barrier_semaphore()

    def signal(s, d):
        pl.semaphore_signal(barrier, inc=1, device_id=(s, d), device_id_type=MESH)

    chips = doms // 2
    reach = chips // 4
    back, ahead = reach, max(reach - 1, 1)
    chip, core = dom // 2, lax.rem(dom, 2)

    def at(offset, c):
        return 2 * lax.rem(chip + offset + chips, chips) + c

    def greet_next(k, c):
        signal(next_sec, at(k // 2 - reach, lax.rem(k, 2)))
        return c

    def greet_back(k, c):
        signal(sec, at(k // 2 - back, lax.rem(k, 2)))
        return c

    def greet_ahead(k, c):
        signal(sec, at(k // 2 + 1, lax.rem(k, 2)))
        return c

    def greet_sec(o, c):
        signal(lax.rem(sec + o, sectors), dom)
        return c

    loads = [
        pltpu.make_async_copy(src, dst, load_sem.at[i])
        for i, (src, dst) in enumerate(
            [
                (velocity_hbm, velocity),
                (load_hbm, load),
                (mobility_hbm, mobility),
                (corner_hbm, corner),
                (strain_hbm, strain),
                (dual_hbm, dual),
                (past_dual_gap_hbm, past_dual_gap),
                (past_velocity_gap_hbm, past_velocity_gap),
                (past_dual_hbm, past_dual),
                (past_velocity_hbm, past_velocity),
            ]
        )
    ]
    loads[0].start()
    lax.fori_loop(0, 2 * (2 * reach + 1), greet_next, 0)
    lax.fori_loop(0, 2 * back, greet_back, 0)
    lax.fori_loop(0, 2 * ahead, greet_ahead, 0)
    signal(sec, at(0, 1 - core))
    lax.fori_loop(2, sectors - 1, greet_sec, 0)
    for l in loads[1:]:
        l.start()

    iota_row = lax.broadcasted_iota(jnp.int32, (8, LANES), 0)
    iota_lane = lax.broadcasted_iota(jnp.int32, (8, LANES), 1)

    speed[...] = jnp.zeros_like(speed)
    load6[...] = jnp.zeros_like(load6)
    for l in loads[0:3]:
        l.wait()
    for j in range(3):
        for h in range(2):
            r, cols = 2 * j + h, pl.ds(LANES * h, LANES)
            speed[0, r : r + 1, :] = velocity[j : j + 1, cols]
            load6[r : r + 1, :] = load[j : j + 1, cols]
    mob6[...] = jnp.where(
        lax.rem(iota_row, 2) == 0,
        jnp.broadcast_to(mobility[0:1, :], (8, LANES)),
        jnp.broadcast_to(mobility[1:2, :], (8, LANES)),
    )

    pl.semaphore_wait(barrier, 2 * (2 * reach + 1) + 2 * (back + ahead) + 1 + (sectors - 3))

    six = pl.ds(0, 6)

    def send_edges(it):
        copy(speed.at[it, six], edge_in.at[it, 0, six], 1 + 2 * it, sec, right).start()
        copy(speed.at[it, six], edge_in.at[it, 1, six], 2 + 2 * it, sec, left).start()

    def wait_edges(it, what):
        getattr(copy(speed.at[it, six], edge_in.at[it, 0, six], 1 + 2 * it, sec, right), what)()
        getattr(copy(speed.at[it, six], edge_in.at[it, 1, six], 2 + 2 * it, sec, left), what)()

    def some_blocks(count, sem):
        block = speed_in.at[0, pl.ds(0, count), six]
        return copy(block, block, sem, prev_sec, dom)

    def relay_copy(offset, sem):
        return copy(speed.at[0, six], speed_in.at[0, dom, six], sem, prev_sec, at(offset, core))

    def send_first():
        def direct(offset, c):
            copy(speed.at[0, six], speed_in.at[0, dom, six], 0, prev_sec, at(offset, c)).start()

        relay_copy(reach, 6).start()
        relay_copy(-reach, 7).start()
        direct(reach, 1 - core)
        direct(-reach, 1 - core)
        for offset in range(reach - 1, -1, -1):
            for o in sorted({offset, -offset}):
                for c in range(2):
                    direct(o, c)
        send_edges(0)

    def pass_on():
        def forward(src, sem, offset, c):
            copy(speed_in.at[0, src, six], speed_in.at[0, src, six], sem, sec, at(offset, c)).start()

        relay_copy(reach, 6).wait_recv()
        for m in range(reach, 0, -1):
            for c in range(2):
                forward(at(-reach, core), 8, m, c)
        relay_copy(-reach, 7).wait_recv()
        for m in range(reach - 1, 0, -1):
            for c in range(2):
                forward(at(reach, core), 8, -m, c)

    def wait_first():
        wait_edges(0, "wait_recv")
        some_blocks(4 * reach, 0).wait_recv()
        some_blocks(2 * (2 * reach - 1), 8).wait_recv()

    def wait_first_sends():
        wait_edges(0, "wait_send")
        relay_copy(reach, 6).wait_send()
        relay_copy(-reach, 7).wait_send()
        some_blocks(4 * reach, 0).wait_send()
        some_blocks(2 * (2 * reach - 1), 8).wait_send()

    def send_second():
        def body(k, c):
            copy(speed.at[1, six], speed_in.at[1, dom, six], 9, prev_sec, far_first(k)).start()
            return c

        lax.fori_loop(0, doms, body, 0)
        send_edges(1)

    def wait_second(what):
        wait_edges(1, what)
        block = speed_in.at[1, :, six]
        getattr(copy(block, block, 9, prev_sec, dom), what)()

    def wait_force(it, what="wait_recv"):
        getattr(copy(force.at[it, doms, six], push_in.at[it, 1, six], 12 + 2 * it, sec, left), what)()
        getattr(copy(force.at[it, doms + 1, six], push_in.at[it, 0, six], 13 + 2 * it, sec, right), what)()
        block = force_in.at[it, :, six]
        getattr(copy(block, block, 10 + it, next_sec, dom), what)()

    seam_copy = copy(seam_hbm, seam_in, 5, prev_sec, dom)
    send_first()
    seam_copy.start()

    for l in loads[3:]:
        l.wait()
    for c in range(3):
        for j in range(3):
            for k in range(4):
                r = 12 * c + 3 * k + j
                for h in range(2):
                    strain_r[3 * c + j, 4 * h + k : 4 * h + k + 1, :] = strain[r : r + 1, pl.ds(LANES * h, LANES)]
    nodes = jnp.concatenate([corner[:, 0:LANES], corner[:, LANES : 2 * LANES]], axis=0)
    slot = LANES * (iota_row // 4) + iota_lane
    alive = jnp.where(slot < counts[0], 1.0, 0.0)
    dual_prev = [
        jnp.where(
            iota_row < 4,
            jnp.broadcast_to(dual[c : c + 1, 0:LANES], (8, LANES)),
            jnp.broadcast_to(dual[c : c + 1, LANES : 2 * LANES], (8, LANES)),
        )
        for c in range(3)
    ]

    pass_on()

    sector_nodes = doms * 2 * LANES
    seam_copy.wait_recv()
    position = nodes - sector_nodes
    place = jnp.bitwise_and(position, LANES - 1)
    place_row = jnp.right_shift(position, 7)
    seam_node = jnp.zeros((8, LANES), jnp.int32)
    for r in range(seam_in.shape[1] // LANES):
        row = jnp.broadcast_to(seam_in[0:1, LANES * r : LANES * (r + 1)], (8, LANES))
        seam_node = jnp.where(place_row == r, lane_take(row, place), seam_node)
    is_seam = position >= 0
    key = jnp.where(is_seam, 4 + jnp.right_shift(seam_node, 7), jnp.right_shift(nodes, 7) - 2 * dom + 1)
    low = jnp.bitwise_and(jnp.where(is_seam, seam_node, nodes), LANES - 1)

    lane_is = lax.broadcasted_iota(jnp.int32, (LANES, LANES), 0)
    for t in range(8):
        hit = lane_is == jnp.broadcast_to(low[t : t + 1, :], (LANES, LANES))
        onehot[:, LANES * t : LANES * (t + 1)] = jnp.where(hit, 1.0, 0.0).astype(jnp.bfloat16)

    half = doms // 2
    wanted = jnp.concatenate([row_bcast(key, t) - jnp.bitwise_and(iota_row, 1) for t in range(8)], axis=1)

    def mark(mask, q, keys):
        pair = jnp.concatenate([jnp.where(wanted == k, 1.0, 0.0) for k in keys], axis=0)
        mask[pl.ds(pl.multiple_of(16 * q, 16), 16), :] = pair.astype(jnp.bfloat16)

    def mark_far(q, c):
        mark(mask_far, q, [4 + 2 * far_first(2 * q + i) for i in range(2)])
        return c

    def mark_near(q, c):
        mark(mask_near, q, [4 + 2 * far_first(half + 2 * q + i) for i in range(2)])
        return c

    lax.fori_loop(0, half // 2, mark_far, 0)
    lax.fori_loop(0, half // 2, mark_near, 0)
    mark(mask_near, half // 2, [0, 2])

    def elements(it, dual_now):
        def look(table, row_key, acc, h):
            out = []
            for j in range(3):
                row = jnp.broadcast_to(table[2 * j + h : 2 * j + h + 1, :], (8, LANES))
                out.append(jnp.where(key == row_key, lane_take(row, low), acc[j]))
            return out

        acc = [jnp.zeros((8, LANES), jnp.float32)] * 3
        acc = look(edge_in.at[it, 0], 0, acc, 1)
        acc = look(speed.at[it], 1, acc, 0)
        acc = look(speed.at[it], 2, acc, 1)
        acc = look(edge_in.at[it, 1], 3, acc, 0)

        for b in range(doms):
            acc = look(speed_in.at[it, b], 4 + 2 * b, acc, 0)
            acc = look(speed_in.at[it, b], 5 + 2 * b, acc, 1)
        rate = []
        for c in range(3):
            part = strain_r[3 * c] * acc[0] + strain_r[3 * c + 1] * acc[1] + strain_r[3 * c + 2] * acc[2]
            rate.append(sum_corners(part, iota_row))
        trial = [rate[c] + dual_now[c] for c in range(3)]
        cone = project_cone(*trial)
        dual_next = [alive * (trial[c] - cone[c]) for c in range(3)]
        misfit = [alive * (rate[c] - cone[c] + dual_next[c]) for c in range(3)]
        push = [
            strain_r[j] * misfit[0] + strain_r[3 + j] * misfit[1] + strain_r[6 + j] * misfit[2] for j in range(3)
        ]
        return dual_next, push

    def spread(it, push):
        split = [[], [], []]
        for t in range(8):
            value = jnp.where(iota_row < 2, row_bcast(push[0], t), row_bcast(push[1], t))
            value = jnp.where(iota_row < 4, value, row_bcast(push[2], t))
            value = jnp.where(iota_row < 6, value, 0.0)
            for s in range(3):
                piece = value.astype(jnp.bfloat16).astype(jnp.float32)
                split[s].append(piece)
                value = value - piece
        split = [jnp.concatenate(p, axis=1) for p in split]
        split = [jnp.concatenate([p, p], axis=0).astype(jnp.bfloat16) for p in split]

        def fill(lhs, mask):
            for q in range(mask.shape[0] // 16):
                rows = slice(16 * q, 16 * q + 16)
                hit = mask[rows, :]
                for s in range(3):
                    lhs[s, rows, :] = hit * split[s]

        def product(lhs):
            rows = lhs.shape[1]
            out = lax.dot_general(
                lhs[...].reshape(3 * rows, 8 * LANES),
                onehot[...],
                (((1,), (1,)), ((), ())),
                preferred_element_type=jnp.float32,
            ).reshape(3, rows // 8, 8, LANES)
            return (out[2] + out[1]) + out[0]

        def send(k, c):
            copy(force.at[it, k, six], force_in.at[it, dom, six], 10 + it, next_sec, far_first(k)).start()
            return c

        fill(lhs_far, mask_far)
        force[it, 0:half] = product(lhs_far)
        lax.fori_loop(0, half, send, 0)
        fill(lhs_near, mask_near)
        force[it, half : doms + 2] = product(lhs_near)
        lax.fori_loop(half, doms, send, 0)
        copy(force.at[it, doms, six], push_in.at[it, 1, six], 12 + 2 * it, sec, left).start()
        copy(force.at[it, doms + 1, six], push_in.at[it, 0, six], 13 + 2 * it, sec, right).start()

    def next_speed(it):
        even = lax.rem(iota_row, 2) == 0
        own = jnp.where(
            even,
            pltpu.roll(force[it, doms] + jnp.where(iota_row < 6, push_in[it, 0], 0.0), 7, 0),
            pltpu.roll(force[it, doms + 1] + jnp.where(iota_row < 6, push_in[it, 1], 0.0), 1, 0),
        )

        def body(b, acc):
            return acc + force_in[it, b]

        own = lax.fori_loop(0, doms, body, own)
        step = speed[it] - mob6[...] * (own - load6[...])
        return jnp.where(iota_row < 6, step, 0.0)

    wait_first()
    dual_one, push = elements(0, dual_prev)
    spread(0, push)
    wait_force(0)
    speed[1] = next_speed(0)
    send_second()
    wait_second("wait_recv")
    dual_two, push = elements(1, dual_one)
    spread(1, push)

    def by_history(ref, j, h):
        return ref[j, :, pl.ds(LANES * h, LANES)]

    depth = 8
    acc = [jnp.zeros((8, LANES), jnp.float32)] * (depth + 1)

    def add_gram(acc, res_row, past):
        res_b = jnp.broadcast_to(res_row, (8, LANES))
        gap = res_b - past
        acc = [acc[i] + gap * row_bcast(gap, i) for i in range(depth)] + [acc[depth] + gap * res_b]
        return acc

    for c in range(3):
        res = dual_two[c] - dual_one[c]
        for h in range(2):
            acc = add_gram(acc, res[4 * h : 4 * h + 1, :], by_history(past_dual_gap, c, h))

    wait_force(1)
    speed_one = speed[1]
    speed_two = next_speed(1)
    res = speed_two - speed_one
    for j in range(3):
        for h in range(2):
            r = 2 * j + h
            acc = add_gram(acc, res[r : r + 1, :], by_history(past_velocity_gap, j, h))
    packed = jnp.zeros((8, LANES), jnp.float32)
    for i in range(depth + 1):
        packed = jnp.where(iota_lane == i, jnp.sum(acc[i], axis=1, keepdims=True), packed)

    def fold(x):
        out = x[0:1, :]
        for l in range(1, 8):
            out = out + pltpu.roll(x[l : l + 1, :], 16 * l, 1)
        return out

    gram_out[0] = fold(packed)

    def send_gram(k, c):
        copy(gram_out.at[0], gram_in.at[k], 16, sec, far_first(k)).start()
        return c

    lax.fori_loop(0, doms - 1, send_gram, 0)
    block = gram_in.at[pl.ds(0, doms - 1)]
    gram_copies = copy(block, block, 16, sec, dom)
    gram_copies.wait_recv()

    def add_in(o, acc):
        return acc + gram_in[o]

    total = lax.fori_loop(0, doms - 1, add_in, gram_out[0])
    total_out[0] = total

    def send_total(o, c):
        copy(total_out.at[0], total_in.at[o], 17, lax.rem(sec + o, sectors), dom).start()
        return c

    lax.fori_loop(1, sectors, send_total, 0)
    block = total_in.at[pl.ds(1, sectors - 1)]
    total_copies = copy(block, block, 17, sec, dom)

    def apart(now_row, past, past_gap):
        return jnp.broadcast_to(now_row, (8, LANES)) - past - past_gap

    parts = [(j, h) for j in range(3) for h in range(2)]
    apart_u = [
        apart(speed_two[2 * j + h : 2 * j + h + 1, :], by_history(past_velocity, j, h), by_history(past_velocity_gap, j, h))
        for j, h in parts
    ]
    apart_w = [
        apart(dual_two[j][4 * h : 4 * h + 1, :], by_history(past_dual, j, h), by_history(past_dual_gap, j, h))
        for j, h in parts
    ]
    seam_copy.wait_send()
    wait_first_sends()
    wait_second("wait_send")
    for it in range(ITERS):
        wait_force(it, "wait_send")
    gram_copies.wait_send()
    total_copies.wait_recv()

    def add_total(o, acc):
        return acc + total_in[o]

    total = lax.fori_loop(1, sectors, add_total, total)

    def entry(lane):
        return jnp.broadcast_to(jnp.broadcast_to(total[:, lane : lane + 1], (1, LANES)), (8, LANES))

    upper = [[entry(16 * i + l) if l >= i else None for l in range(depth + 1)] for i in range(depth)]
    trace = upper[0][0]
    for i in range(1, depth):
        trace = trace + upper[i][i]
    ridge = 0.0001 * trace / depth
    for i in range(depth):
        upper[i][i] = upper[i][i] + ridge
    inverse = []
    for k in range(depth):
        inverse.append(1.0 / upper[k][k])
        for i in range(k + 1, depth):
            scale = upper[k][i] * inverse[k]
            for l in range(i, depth + 1):
                upper[i][l] = upper[i][l] - scale * upper[k][l]
    solved = [None] * depth
    for k in reversed(range(depth)):
        value = upper[k][depth]
        for l in range(k + 1, depth):
            value = value - upper[k][l] * solved[l]
        solved[k] = value * inverse[k]
    coeffs = solved[0]
    for i in range(1, depth):
        coeffs = jnp.where(iota_row == i, solved[i], coeffs)

    for p, (j, h) in enumerate(parts):
        cols = pl.ds(LANES * h, LANES)
        result[j : j + 1, cols] = speed_two[2 * j + h : 2 * j + h + 1, :] - jnp.sum(
            coeffs * apart_u[p], axis=0, keepdims=True
        )
        result[4 + j : 5 + j, cols] = dual_two[j][4 * h : 4 * h + 1, :] - jnp.sum(
            coeffs * apart_w[p], axis=0, keepdims=True
        )
    total_copies.wait_send()


def per_device(
    strain_map,
    corner_nodes,
    counts,
    seam_nodes,
    velocity,
    dual_state,
    nodal_load,
    mobility,
    past_dual,
    past_dual_gap,
    past_velocity,
    past_velocity_gap,
):
    sectors, doms = lax.axis_size("sector"), lax.axis_size("dom")
    out = jax.ShapeDtypeStruct(velocity.shape, jnp.float32)
    vmem = pl.BlockSpec(memory_space=pltpu.VMEM)
    smem = pl.BlockSpec(memory_space=pltpu.SMEM)
    hbm = pl.BlockSpec(memory_space=pl.ANY)
    history = pltpu.VMEM((3, 8, 2 * LANES), jnp.float32)
    f32 = jnp.float32
    result = pl.pallas_call(
        functools.partial(kernel, sectors, doms),
        out_shape=pltpu.VMEM((8, 2 * LANES), f32),
        in_specs=[hbm, hbm, smem] + [hbm] * 9,
        out_specs=vmem,
        scratch_shapes=[
            pltpu.VMEM(strain_map.shape, f32),
            pltpu.VMEM(corner_nodes.shape, jnp.int32),
            pltpu.VMEM(velocity.shape, f32),
            pltpu.VMEM(dual_state.shape, f32),
            pltpu.VMEM(nodal_load.shape, f32),
            pltpu.VMEM((2, LANES), f32),
            history,
            history,
            history,
            history,
            pltpu.VMEM((2, 8, LANES), f32),
            pltpu.VMEM((8, LANES), f32),
            pltpu.VMEM((8, LANES), f32),
            pltpu.VMEM((9, 8, LANES), f32),
            pltpu.VMEM(seam_nodes.shape, jnp.int32),
            pltpu.VMEM((2, doms, 8, LANES), f32),
            pltpu.VMEM((2, 2, 8, LANES), f32),
            pltpu.VMEM((2, doms + 2, 8, LANES), f32),
            pltpu.VMEM((2, doms, 8, LANES), f32),
            pltpu.VMEM((2, 2, 8, LANES), f32),
            pltpu.VMEM((LANES, 8 * LANES), jnp.bfloat16),
            pltpu.VMEM((3, 4 * doms, 8 * LANES), jnp.bfloat16),
            pltpu.VMEM((3, 4 * doms + 16, 8 * LANES), jnp.bfloat16),
            pltpu.VMEM((1, 1, LANES), f32),
            pltpu.VMEM((doms, 1, LANES), f32),
            pltpu.VMEM((1, 1, LANES), f32),
            pltpu.VMEM((sectors, 1, LANES), f32),
            pltpu.VMEM((4 * doms, 8 * LANES), jnp.bfloat16),
            pltpu.VMEM((4 * doms + 16, 8 * LANES), jnp.bfloat16),
            pltpu.SemaphoreType.DMA((10,)),
            pltpu.SemaphoreType.DMA((18,)),
            pltpu.SemaphoreType.DMA((18,)),
        ],
        compiler_params=pltpu.CompilerParams(collective_id=0, has_side_effects=True),
        name="dome",
    )(
        strain_map,
        corner_nodes,
        counts,
        seam_nodes,
        velocity,
        dual_state,
        nodal_load,
        mobility.reshape(2, LANES),
        past_dual.transpose(1, 0, 2),
        past_dual_gap.transpose(1, 0, 2),
        past_velocity.transpose(1, 0, 2),
        past_velocity_gap.transpose(1, 0, 2),
    )
    return result[0:3], result[4:7]


def solution(mesh):
    part = ("sector", "dom")
    in_specs = (
        P(None, part),
        P(None, part),
        P(part),
        P("sector", None),
        P(None, part),
        P(None, part),
        P(None, part),
        P(part),
        P(None, None, part),
        P(None, None, part),
        P(None, None, part),
        P(None, None, part),
    )
    out_specs = (P(None, part), P(None, part))
    return jax.shard_map(per_device, mesh=mesh, in_specs=in_specs, out_specs=out_specs, check_vma=False)
```

```python
import functools

import jax
import jax.numpy as jnp
from jax import lax
from jax.experimental import pallas as pl
from jax.experimental.pallas import tpu as pltpu
from jax.sharding import PartitionSpec as P

MESH = pl.DeviceIdType.MESH
ITERS = 2
LANES = 128


def row_bcast(x, r):
    return jnp.broadcast_to(x[r : r + 1, :], (8, LANES))


def lane_take(row, index):
    return jnp.take_along_axis(row, index, axis=1, mode="promise_in_bounds")


def sum_corners(x, iota_row):
    odd = lax.rem(iota_row, 2) == 1
    x = x + jnp.where(odd, pltpu.roll(x, 1, 0), pltpu.roll(x, 7, 0))
    high = lax.rem(iota_row, 4) >= 2
    return x + jnp.where(high, pltpu.roll(x, 2, 0), pltpu.roll(x, 6, 0))


def project_cone(a, b, shear):
    center = 0.5 * (a + b)
    spread = 0.5 * (a - b)
    radius = jnp.sqrt(spread * spread + shear * shear)
    upper = center + radius
    lower = center - radius
    iso_part = 0.5 * (jnp.maximum(upper, 0.0) + jnp.maximum(lower, 0.0))
    factor = jnp.clip(upper / (2.0 * jnp.maximum(radius, 0.05)), 0.0, 1.0)
    return iso_part + factor * spread, iso_part - factor * spread, factor * shear


def kernel(
    sectors,
    doms,
    strain_hbm,
    corner_hbm,
    counts_hbm,
    seam_hbm,
    velocity_hbm,
    dual_hbm,
    load_hbm,
    mobility_hbm,
    past_dual_hbm,
    past_dual_gap_hbm,
    past_velocity_hbm,
    past_velocity_gap_hbm,
    result,
    counts,
    strain,
    corner,
    velocity,
    dual,
    load,
    mobility,
    past_dual,
    past_dual_gap,
    past_velocity,
    past_velocity_gap,
    speed,
    load6,
    mob6,
    strain_r,
    own_seam,
    seam_in,
    base_out,
    base_in,
    own_out,
    own_in,
    seam_out,
    seam_part,
    seam_speed,
    speed_in,
    edge_in,
    force,
    force_in,
    push_in,
    onehot,
    lhs_far,
    lhs_near,
    gram_out,
    gram_in,
    total_out,
    total_in,
    mask_far,
    mask_near,
    load_sem,
    ready,
    send_sem,
    recv_sem,
):
    sec = lax.axis_index("sector")
    dom = lax.axis_index("dom")
    prev_sec = lax.rem(sec + sectors - 1, sectors)
    next_sec = lax.rem(sec + 1, sectors)
    left = lax.rem(dom + doms - 1, doms)
    right = lax.rem(dom + 1, doms)

    def copy(src, dst, sem, s, d):
        return pltpu.make_async_remote_copy(
            src_ref=src,
            dst_ref=dst,
            send_sem=send_sem.at[sem],
            recv_sem=recv_sem.at[sem],
            device_id=(s, d),
            device_id_type=MESH,
        )

    def far_first(k):
        step = (k + 1) // 2
        return lax.rem(dom + doms // 2 + jnp.where(lax.rem(k, 2) == 1, doms - step, step), doms)

    barrier = pltpu.get_barrier_semaphore()

    def signal(s, d):
        pl.semaphore_signal(barrier, inc=1, device_id=(s, d), device_id_type=MESH)

    chips = doms // 2
    reach = chips // 4
    back, ahead = reach, reach
    chip, core = dom // 2, lax.rem(dom, 2)

    def at(offset, c):
        return 2 * lax.rem(chip + offset + chips, chips) + c

    def greet_next(k, c):
        signal(next_sec, at(k // 2 - reach, lax.rem(k, 2)))
        return c

    def greet_back(k, c):
        signal(sec, at(k // 2 - back, lax.rem(k, 2)))
        return c

    def greet_ahead(k, c):
        signal(sec, at(k // 2 + 1, lax.rem(k, 2)))
        return c

    def greet_sec(o, c):
        signal(lax.rem(sec + o, sectors), dom)
        return c

    loads = [
        pltpu.make_async_copy(src, dst, load_sem.at[i])
        for i, (src, dst) in enumerate(
            [
                (velocity_hbm, velocity),
                (load_hbm, load),
                (mobility_hbm, mobility),
                (corner_hbm, corner),
                (strain_hbm, strain),
                (dual_hbm, dual),
                (past_dual_gap_hbm, past_dual_gap),
                (past_velocity_gap_hbm, past_velocity_gap),
                (past_dual_hbm, past_dual),
                (past_velocity_hbm, past_velocity),
                (counts_hbm, counts),
                (seam_hbm, own_seam),
            ]
        )
    ]
    loads[0].start()
    lax.fori_loop(0, 2 * (2 * reach + 1), greet_next, 0)
    lax.fori_loop(0, 2 * back, greet_back, 0)
    lax.fori_loop(0, 2 * ahead, greet_ahead, 0)
    signal(sec, at(0, 1 - core))
    lax.fori_loop(2, sectors - 1, greet_sec, 0)
    for l in loads[1:]:
        l.start()

    iota_row = lax.broadcasted_iota(jnp.int32, (8, LANES), 0)
    iota_lane = lax.broadcasted_iota(jnp.int32, (8, LANES), 1)

    speed[...] = jnp.zeros_like(speed)
    load6[...] = jnp.zeros_like(load6)
    for l in loads[0:3]:
        l.wait()
    for j in range(3):
        for h in range(2):
            r, cols = 2 * j + h, pl.ds(LANES * h, LANES)
            speed[0, r : r + 1, :] = velocity[j : j + 1, cols]
            load6[r : r + 1, :] = load[j : j + 1, cols]
    mob6[...] = jnp.where(
        lax.rem(iota_row, 2) == 0,
        jnp.broadcast_to(mobility[0:1, :], (8, LANES)),
        jnp.broadcast_to(mobility[1:2, :], (8, LANES)),
    )

    pl.semaphore_wait(barrier, 2 * (2 * reach + 1) + 2 * (back + ahead) + 1 + (sectors - 3))

    six = pl.ds(0, 6)

    def send_edges(it):
        copy(speed.at[it, six], edge_in.at[it, 0, six], 1 + 2 * it, sec, right).start()
        copy(speed.at[it, six], edge_in.at[it, 1, six], 2 + 2 * it, sec, left).start()

    def wait_edges(it, what):
        getattr(copy(speed.at[it, six], edge_in.at[it, 0, six], 1 + 2 * it, sec, right), what)()
        getattr(copy(speed.at[it, six], edge_in.at[it, 1, six], 2 + 2 * it, sec, left), what)()

    def some_blocks(count, sem):
        block = speed_in.at[0, pl.ds(0, count), six]
        return copy(block, block, sem, prev_sec, dom)

    def relay_copy(offset, sem):
        return copy(speed.at[0, six], speed_in.at[0, dom, six], sem, prev_sec, at(offset, core))

    def send_first():
        def direct(offset, c):
            copy(speed.at[0, six], speed_in.at[0, dom, six], 0, prev_sec, at(offset, c)).start()

        relay_copy(reach, 6).start()
        relay_copy(-reach, 7).start()
        direct(reach, 1 - core)
        direct(-reach, 1 - core)
        for offset in range(reach - 1, -1, -1):
            for o in sorted({offset, -offset}):
                for c in range(2):
                    direct(o, c)
        send_edges(0)

    def pass_on():
        def forward(src, sem, offset, c):
            copy(speed_in.at[0, src, six], speed_in.at[0, src, six], sem, sec, at(offset, c)).start()

        def answer(offset):
            pl.semaphore_signal(ready, inc=1, device_id=(next_sec, at(offset, core)), device_id_type=MESH)

        relay_copy(reach, 6).wait_recv()
        answer(-reach)
        for m in range(reach, 0, -1):
            for c in range(2):
                forward(at(-reach, core), 8, m, c)
        relay_copy(-reach, 7).wait_recv()
        answer(reach)
        for m in range(reach - 1, 0, -1):
            for c in range(2):
                forward(at(reach, core), 8, -m, c)

    def wait_first():
        wait_edges(0, "wait_recv")
        some_blocks(4 * reach, 0).wait_recv()
        some_blocks(2 * (2 * reach - 1), 8).wait_recv()

    def wait_first_sends():
        wait_edges(0, "wait_send")
        relay_copy(reach, 6).wait_send()
        relay_copy(-reach, 7).wait_send()
        some_blocks(4 * reach, 0).wait_send()
        some_blocks(2 * (2 * reach - 1), 8).wait_send()

    def all_small(ref, count, sem):
        block = ref.at[pl.ds(0, count)]
        return copy(block, block, sem, sec, dom)

    def small_wait(i, what):
        ref, count, sem = [(base_in, doms, 18), (own_in, doms, 19), (seam_part, doms - 1, 20), (seam_speed, doms - 1, 9)][i]
        getattr(all_small(ref, count, sem), what)()

    def send_base(k, c):
        d = far_first(k)
        copy(base_out.at[d], base_in.at[dom], 18, prev_sec, d).start()
        return c

    def send_own(k, c):
        d = far_first(k)
        copy(own_out.at[d], own_in.at[dom], 19, prev_sec, d).start()
        return c

    def send_seam(k, c):
        d = far_first(k)
        copy(seam_out.at[d], seam_part.at[dom], 20, sec, d).start()
        return c

    def send_seam_speed(k, c):
        copy(seam_speed.at[dom], seam_speed.at[dom], 9, sec, far_first(k)).start()
        return c

    def wait_force(it, what="wait_recv"):
        getattr(copy(force.at[it, doms, six], push_in.at[it, 1, six], 12 + 2 * it, sec, left), what)()
        getattr(copy(force.at[it, doms + 1, six], push_in.at[it, 0, six], 13 + 2 * it, sec, right), what)()
        block = force_in.at[it, :, six]
        getattr(copy(block, block, 10 + it, next_sec, dom), what)()

    for offset in (reach, -reach):
        pl.semaphore_signal(ready, inc=1, device_id=(sec, at(offset, core)), device_id_type=MESH)

    seam_copy = copy(seam_hbm, seam_in, 5, prev_sec, dom)
    send_first()
    seam_copy.start()

    for l in loads[3:]:
        l.wait()
    for c in range(3):
        for j in range(3):
            for k in range(4):
                r = 12 * c + 3 * k + j
                for h in range(2):
                    strain_r[3 * c + j, 4 * h + k : 4 * h + k + 1, :] = strain[r : r + 1, pl.ds(LANES * h, LANES)]
    nodes = jnp.concatenate([corner[:, 0:LANES], corner[:, LANES : 2 * LANES]], axis=0)
    slot = LANES * (iota_row // 4) + iota_lane
    alive = jnp.where(slot < counts[0], 1.0, 0.0)
    dual_prev = [
        jnp.where(
            iota_row < 4,
            jnp.broadcast_to(dual[c : c + 1, 0:LANES], (8, LANES)),
            jnp.broadcast_to(dual[c : c + 1, LANES : 2 * LANES], (8, LANES)),
        )
        for c in range(3)
    ]

    pass_on()

    sector_nodes = doms * 2 * LANES
    seam_copy.wait_recv()
    position = nodes - sector_nodes
    place = jnp.bitwise_and(position, LANES - 1)
    place_row = jnp.right_shift(position, 7)
    seam_node = jnp.zeros((8, LANES), jnp.int32)
    for r in range(seam_in.shape[1] // LANES):
        row = jnp.broadcast_to(seam_in[0:1, LANES * r : LANES * (r + 1)], (8, LANES))
        seam_node = jnp.where(place_row == r, lane_take(row, place), seam_node)
    is_seam = position >= 0
    key = jnp.where(is_seam, 4 + jnp.right_shift(seam_node, 7), jnp.right_shift(nodes, 7) - 2 * dom + 1)
    low = jnp.bitwise_and(jnp.where(is_seam, seam_node, nodes), LANES - 1)

    lane_is = lax.broadcasted_iota(jnp.int32, (LANES, LANES), 0)
    for t in range(8):
        hit = lane_is == jnp.broadcast_to(low[t : t + 1, :], (LANES, LANES))
        onehot[:, LANES * t : LANES * (t + 1)] = jnp.where(hit, 1.0, 0.0).astype(jnp.bfloat16)

    half = doms // 2
    wanted = jnp.concatenate([row_bcast(key, t) - jnp.bitwise_and(iota_row, 1) for t in range(8)], axis=1)

    def mark(mask, q, keys):
        pair = jnp.concatenate([jnp.where(wanted == k, 1.0, 0.0) for k in keys], axis=0)
        mask[pl.ds(pl.multiple_of(16 * q, 16), 16), :] = pair.astype(jnp.bfloat16)

    def mark_far(q, c):
        mark(mask_far, q, [4 + 2 * far_first(2 * q + i) for i in range(2)])
        return c

    def mark_near(q, c):
        mark(mask_near, q, [4 + 2 * far_first(half + 2 * q + i) for i in range(2)])
        return c

    lax.fori_loop(0, half // 2, mark_far, 0)
    lax.fori_loop(0, half // 2, mark_near, 0)
    mark(mask_near, half // 2, [0, 2])

    low_half = iota_lane < LANES // 2
    groups = own_seam.shape[1] // (8 * LANES)

    def positions(ref, g):
        rows = [ref[0:1, LANES * (8 * g + r) : LANES * (8 * g + r + 1)] for r in range(8)]
        node = jnp.concatenate(rows, axis=0)
        return jnp.right_shift(node, 7), jnp.bitwise_and(node, LANES - 1)

    def swap(x):
        return pltpu.roll(x, LANES // 2, 1)

    def write_messages(ref, g, first, second, third, fourth):
        even = (jnp.where(low_half, first, swap(second)), jnp.where(low_half, third, swap(fourth)))
        odd = (jnp.where(low_half, swap(first), second), jnp.where(low_half, swap(third), fourth))
        for r in range(8):
            for parity, rows in enumerate((even, odd)):
                for i in range(2):
                    ref[2 * (8 * g + r) + parity, i : i + 1, :] = rows[i][r : r + 1, :]

    zero = jnp.zeros((8, LANES), jnp.float32)
    base6 = speed[0] + mob6[...] * load6[...]
    for g in range(groups):
        node_row, node_lane = positions(own_seam, g)
        found = [zero] * 4
        for h in range(2):
            hit = node_row == 2 * dom + h
            for j in range(4):
                row = row_bcast(base6, 2 * j + h) if j < 3 else row_bcast(mob6[...], h)
                found[j] = jnp.where(hit, lane_take(row, node_lane), found[j])
        write_messages(base_out, g, *found)

    def seam_forces():
        for g in range(groups):
            node_row, node_lane = positions(seam_in, g)
            found = [zero] * 3
            for k in range(doms):
                block = force[0, k]
                for h in range(2):
                    hit = node_row == 2 * far_first(k) + h
                    for j in range(3):
                        found[j] = jnp.where(hit, lane_take(row_bcast(block, 2 * j + h), node_lane), found[j])
            write_messages(seam_out, g, *found, zero)

    def own_forces():
        for g in range(groups):
            node_row, node_lane = positions(own_seam, g)
            found = [zero] * 3
            for row_key in range(4):
                block = force[0, doms + row_key // 2]
                hit = node_row - 2 * dom + 1 == row_key
                for j in range(3):
                    row = row_bcast(block, 2 * j + row_key % 2)
                    found[j] = jnp.where(hit, lane_take(row, node_lane), found[j])
            write_messages(own_out, g, *found, zero)

    def sum_blocks(refs):
        group = [ref[b] for ref in refs for b in range(doms)]
        while len(group) > 1:
            group = [x + y for x, y in zip(group[::2], group[1::2])] + group[len(group) - len(group) % 2 :]
        return group[0]

    def collect():
        seam_part[dom] = seam_out[dom]
        small_wait(0, "wait_recv")
        base = sum_blocks([base_in])
        half_lane = lax.broadcasted_iota(jnp.int32, (2, LANES), 1) < LANES // 2
        last = jnp.broadcast_to(base[1:2, :], (2, LANES))
        step = jnp.where(half_lane, pltpu.roll(last, LANES // 2, 1), last)
        small_wait(1, "wait_recv")
        small_wait(2, "wait_recv")
        seam_speed[dom] = base - step * sum_blocks([own_in, seam_part])
        lax.fori_loop(0, doms - 1, send_seam_speed, 0)

    collector = jnp.where(is_seam, jnp.right_shift(position, 6), -1)
    place_low = jnp.bitwise_and(position, LANES // 2 - 1)

    def elements(it, dual_now):
        def look(table, row_key, acc, h):
            out = []
            for j in range(3):
                row = jnp.broadcast_to(table[2 * j + h : 2 * j + h + 1, :], (8, LANES))
                out.append(jnp.where(key == row_key, lane_take(row, low), acc[j]))
            return out

        acc = [jnp.zeros((8, LANES), jnp.float32)] * 3
        acc = look(edge_in.at[it, 0], 0, acc, 1)
        acc = look(speed.at[it], 1, acc, 0)
        acc = look(speed.at[it], 2, acc, 1)
        acc = look(edge_in.at[it, 1], 3, acc, 0)

        for b in range(doms):
            if it == 0:
                acc = look(speed_in.at[it, b], 4 + 2 * b, acc, 0)
                acc = look(speed_in.at[it, b], 5 + 2 * b, acc, 1)
            else:
                hit = collector == b
                rows = [jnp.broadcast_to(seam_speed[b, i : i + 1, :], (8, LANES)) for i in range(2)]
                picks = [(rows[0], place_low), (rows[0], place_low + LANES // 2), (rows[1], place_low)]
                acc = [jnp.where(hit, lane_take(*pick), x) for pick, x in zip(picks, acc)]
        rate = []
        for c in range(3):
            part = strain_r[3 * c] * acc[0] + strain_r[3 * c + 1] * acc[1] + strain_r[3 * c + 2] * acc[2]
            rate.append(sum_corners(part, iota_row))
        trial = [rate[c] + dual_now[c] for c in range(3)]
        cone = project_cone(*trial)
        dual_next = [alive * (trial[c] - cone[c]) for c in range(3)]
        misfit = [alive * (rate[c] - cone[c] + dual_next[c]) for c in range(3)]
        push = [
            strain_r[j] * misfit[0] + strain_r[3 + j] * misfit[1] + strain_r[6 + j] * misfit[2] for j in range(3)
        ]
        return dual_next, push

    def spread(it, push):
        split = [[], [], []]
        for t in range(8):
            value = jnp.where(iota_row < 2, row_bcast(push[0], t), row_bcast(push[1], t))
            value = jnp.where(iota_row < 4, value, row_bcast(push[2], t))
            value = jnp.where(iota_row < 6, value, 0.0)
            for s in range(3):
                piece = value.astype(jnp.bfloat16).astype(jnp.float32)
                split[s].append(piece)
                value = value - piece
        split = [jnp.concatenate(p, axis=1) for p in split]
        split = [jnp.concatenate([p, p], axis=0).astype(jnp.bfloat16) for p in split]

        def fill(lhs, mask):
            for q in range(mask.shape[0] // 16):
                rows = slice(16 * q, 16 * q + 16)
                hit = mask[rows, :]
                for s in range(3):
                    lhs[s, rows, :] = hit * split[s]

        def product(lhs):
            rows = lhs.shape[1]
            out = lax.dot_general(
                lhs[...].reshape(3 * rows, 8 * LANES),
                onehot[...],
                (((1,), (1,)), ((), ())),
                preferred_element_type=jnp.float32,
            ).reshape(3, rows // 8, 8, LANES)
            return (out[2] + out[1]) + out[0]

        def send(k, c):
            copy(force.at[it, k, six], force_in.at[it, dom, six], 10 + it, next_sec, far_first(k)).start()
            return c

        fill(lhs_far, mask_far)
        force[it, 0:half] = product(lhs_far)
        if it == 1:
            lax.fori_loop(0, half, send, 0)
        fill(lhs_near, mask_near)
        force[it, half : doms + 2] = product(lhs_near)
        if it == 0:
            own_forces()
            lax.fori_loop(0, doms, send_own, 0)
            seam_forces()
            lax.fori_loop(0, doms - 1, send_seam, 0)
            lax.fori_loop(0, half, send, 0)
        lax.fori_loop(half, doms, send, 0)
        copy(force.at[it, doms, six], push_in.at[it, 1, six], 12 + 2 * it, sec, left).start()
        copy(force.at[it, doms + 1, six], push_in.at[it, 0, six], 13 + 2 * it, sec, right).start()

    def next_speed(it):
        even = lax.rem(iota_row, 2) == 0
        own = jnp.where(
            even,
            pltpu.roll(force[it, doms] + jnp.where(iota_row < 6, push_in[it, 0], 0.0), 7, 0),
            pltpu.roll(force[it, doms + 1] + jnp.where(iota_row < 6, push_in[it, 1], 0.0), 1, 0),
        )

        for b in range(0, doms, 8):
            group = [force_in[it, b + i] for i in range(8)]
            while len(group) > 1:
                group = [x + y for x, y in zip(group[::2], group[1::2])]
            own = own + group[0]
        step = speed[it] - mob6[...] * (own - load6[...])
        return jnp.where(iota_row < 6, step, 0.0)

    wait_first()
    pl.semaphore_wait(ready, 4)
    lax.fori_loop(0, doms, send_base, 0)
    dual_one, push = elements(0, dual_prev)
    spread(0, push)
    collect()
    wait_force(0)
    speed[1] = next_speed(0)
    send_edges(1)
    wait_edges(1, "wait_recv")
    small_wait(3, "wait_recv")
    dual_two, push = elements(1, dual_one)
    spread(1, push)

    def by_history(ref, j, h):
        return ref[j, :, pl.ds(LANES * h, LANES)]

    depth = 8
    acc = [jnp.zeros((8, LANES), jnp.float32)] * (depth + 1)

    def add_gram(acc, res_row, past):
        res_b = jnp.broadcast_to(res_row, (8, LANES))
        gap = res_b - past
        acc = [acc[i] + gap * row_bcast(gap, i) for i in range(depth)] + [acc[depth] + gap * res_b]
        return acc

    for c in range(3):
        res = dual_two[c] - dual_one[c]
        for h in range(2):
            acc = add_gram(acc, res[4 * h : 4 * h + 1, :], by_history(past_dual_gap, c, h))

    wait_force(1)
    speed_one = speed[1]
    speed_two = next_speed(1)
    res = speed_two - speed_one
    for j in range(3):
        for h in range(2):
            r = 2 * j + h
            acc = add_gram(acc, res[r : r + 1, :], by_history(past_velocity_gap, j, h))
    packed = jnp.zeros((8, LANES), jnp.float32)
    for i in range(depth + 1):
        packed = jnp.where(iota_lane == i, jnp.sum(acc[i], axis=1, keepdims=True), packed)

    def fold(x):
        out = x[0:1, :]
        for l in range(1, 8):
            out = out + pltpu.roll(x[l : l + 1, :], 16 * l, 1)
        return out

    gram_out[0] = fold(packed)

    def send_gram(k, c):
        copy(gram_out.at[0], gram_in.at[k], 16, sec, far_first(k)).start()
        return c

    lax.fori_loop(0, doms - 1, send_gram, 0)
    block = gram_in.at[pl.ds(0, doms - 1)]
    gram_copies = copy(block, block, 16, sec, dom)
    gram_copies.wait_recv()

    def add_all(own, ref, first, last):
        group = [own] + [ref[o] for o in range(first, last)]
        while len(group) > 1:
            group = [x + y for x, y in zip(group[::2], group[1::2])] + group[len(group) - len(group) % 2 :]
        return group[0]

    total = add_all(gram_out[0], gram_in, 0, doms - 1)
    total_out[0] = total

    def send_total(o, c):
        copy(total_out.at[0], total_in.at[o], 17, lax.rem(sec + o, sectors), dom).start()
        return c

    lax.fori_loop(1, sectors, send_total, 0)
    block = total_in.at[pl.ds(1, sectors - 1)]
    total_copies = copy(block, block, 17, sec, dom)

    def apart(now_row, past, past_gap):
        return jnp.broadcast_to(now_row, (8, LANES)) - past - past_gap

    parts = [(j, h) for j in range(3) for h in range(2)]
    apart_u = [
        apart(speed_two[2 * j + h : 2 * j + h + 1, :], by_history(past_velocity, j, h), by_history(past_velocity_gap, j, h))
        for j, h in parts
    ]
    apart_w = [
        apart(dual_two[j][4 * h : 4 * h + 1, :], by_history(past_dual, j, h), by_history(past_dual_gap, j, h))
        for j, h in parts
    ]
    seam_copy.wait_send()
    wait_first_sends()
    wait_edges(1, "wait_send")
    for i in range(4):
        small_wait(i, "wait_send")
    for it in range(ITERS):
        wait_force(it, "wait_send")
    gram_copies.wait_send()
    total_copies.wait_recv()

    total = add_all(total, total_in, 1, sectors)

    def entry(lane):
        return jnp.broadcast_to(jnp.broadcast_to(total[:, lane : lane + 1], (1, LANES)), (8, LANES))

    upper = [[entry(16 * i + l) if l >= i else None for l in range(depth + 1)] for i in range(depth)]
    trace = upper[0][0]
    for i in range(1, depth):
        trace = trace + upper[i][i]
    ridge = 0.0001 * trace / depth
    for i in range(depth):
        upper[i][i] = upper[i][i] + ridge
    inverse = []
    for k in range(depth):
        inverse.append(1.0 / upper[k][k])
        for i in range(k + 1, depth):
            scale = upper[k][i] * inverse[k]
            for l in range(i, depth + 1):
                upper[i][l] = upper[i][l] - scale * upper[k][l]
    solved = [None] * depth
    for k in reversed(range(depth)):
        value = upper[k][depth]
        for l in range(k + 1, depth):
            value = value - upper[k][l] * solved[l]
        solved[k] = value * inverse[k]
    coeffs = solved[0]
    for i in range(1, depth):
        coeffs = jnp.where(iota_row == i, solved[i], coeffs)

    for p, (j, h) in enumerate(parts):
        cols = pl.ds(LANES * h, LANES)
        result[j : j + 1, cols] = speed_two[2 * j + h : 2 * j + h + 1, :] - jnp.sum(
            coeffs * apart_u[p], axis=0, keepdims=True
        )
        result[4 + j : 5 + j, cols] = dual_two[j][4 * h : 4 * h + 1, :] - jnp.sum(
            coeffs * apart_w[p], axis=0, keepdims=True
        )
    total_copies.wait_send()


def per_device(
    strain_map,
    corner_nodes,
    counts,
    seam_nodes,
    velocity,
    dual_state,
    nodal_load,
    mobility,
    past_dual,
    past_dual_gap,
    past_velocity,
    past_velocity_gap,
):
    sectors, doms = lax.axis_size("sector"), lax.axis_size("dom")
    out = jax.ShapeDtypeStruct(velocity.shape, jnp.float32)
    vmem = pl.BlockSpec(memory_space=pltpu.VMEM)
    hbm = pl.BlockSpec(memory_space=pl.ANY)
    history = pltpu.VMEM((3, 8, 2 * LANES), jnp.float32)
    small = pltpu.VMEM((doms, 2, LANES), jnp.float32)
    f32 = jnp.float32
    result = pl.pallas_call(
        functools.partial(kernel, sectors, doms),
        out_shape=pltpu.VMEM((8, 2 * LANES), f32),
        in_specs=[hbm] * 12,
        out_specs=vmem,
        scratch_shapes=[
            pltpu.SMEM(counts.shape, jnp.int32),
            pltpu.VMEM(strain_map.shape, f32),
            pltpu.VMEM(corner_nodes.shape, jnp.int32),
            pltpu.VMEM(velocity.shape, f32),
            pltpu.VMEM(dual_state.shape, f32),
            pltpu.VMEM(nodal_load.shape, f32),
            pltpu.VMEM((2, LANES), f32),
            history,
            history,
            history,
            history,
            pltpu.VMEM((2, 8, LANES), f32),
            pltpu.VMEM((8, LANES), f32),
            pltpu.VMEM((8, LANES), f32),
            pltpu.VMEM((9, 8, LANES), f32),
            pltpu.VMEM(seam_nodes.shape, jnp.int32),
            pltpu.VMEM(seam_nodes.shape, jnp.int32),
            small,
            small,
            small,
            small,
            small,
            small,
            small,
            pltpu.VMEM((1, doms, 8, LANES), f32),
            pltpu.VMEM((2, 2, 8, LANES), f32),
            pltpu.VMEM((2, doms + 2, 8, LANES), f32),
            pltpu.VMEM((2, doms, 8, LANES), f32),
            pltpu.VMEM((2, 2, 8, LANES), f32),
            pltpu.VMEM((LANES, 8 * LANES), jnp.bfloat16),
            pltpu.VMEM((3, 4 * doms, 8 * LANES), jnp.bfloat16),
            pltpu.VMEM((3, 4 * doms + 16, 8 * LANES), jnp.bfloat16),
            pltpu.VMEM((1, 1, LANES), f32),
            pltpu.VMEM((doms, 1, LANES), f32),
            pltpu.VMEM((1, 1, LANES), f32),
            pltpu.VMEM((sectors, 1, LANES), f32),
            pltpu.VMEM((4 * doms, 8 * LANES), jnp.bfloat16),
            pltpu.VMEM((4 * doms + 16, 8 * LANES), jnp.bfloat16),
            pltpu.SemaphoreType.DMA((12,)),
            pltpu.SemaphoreType.REGULAR,
            pltpu.SemaphoreType.DMA((21,)),
            pltpu.SemaphoreType.DMA((21,)),
        ],
        compiler_params=pltpu.CompilerParams(collective_id=0, has_side_effects=True),
        name="dome",
    )(
        strain_map,
        corner_nodes,
        counts,
        seam_nodes,
        velocity,
        dual_state,
        nodal_load,
        mobility.reshape(2, LANES),
        past_dual.transpose(1, 0, 2),
        past_dual_gap.transpose(1, 0, 2),
        past_velocity.transpose(1, 0, 2),
        past_velocity_gap.transpose(1, 0, 2),
    )
    return result[0:3], result[4:7]


def solution(mesh):
    part = ("sector", "dom")
    in_specs = (
        P(None, part),
        P(None, part),
        P(part),
        P("sector", None),
        P(None, part),
        P(None, part),
        P(None, part),
        P(part),
        P(None, None, part),
        P(None, None, part),
        P(None, None, part),
        P(None, None, part),
    )
    out_specs = (P(None, part), P(None, part))
    return jax.shard_map(per_device, mesh=mesh, in_specs=in_specs, out_specs=out_specs, check_vma=False)
```

```python
import functools

import jax
import jax.numpy as jnp
from jax import lax
from jax.experimental import pallas as pl
from jax.experimental.pallas import tpu as pltpu
from jax.sharding import PartitionSpec as P

MESH = pl.DeviceIdType.MESH
ITERS = 2
LANES = 128


def row_bcast(x, r):
    return jnp.broadcast_to(x[r : r + 1, :], (8, LANES))


def lane_take(row, index):
    return jnp.take_along_axis(row, index, axis=1, mode="promise_in_bounds")


def sum_corners(x, iota_row):
    odd = lax.rem(iota_row, 2) == 1
    x = x + jnp.where(odd, pltpu.roll(x, 1, 0), pltpu.roll(x, 7, 0))
    high = lax.rem(iota_row, 4) >= 2
    return x + jnp.where(high, pltpu.roll(x, 2, 0), pltpu.roll(x, 6, 0))


def project_cone(a, b, shear):
    center = 0.5 * (a + b)
    spread = 0.5 * (a - b)
    radius = jnp.sqrt(spread * spread + shear * shear)
    upper = center + radius
    lower = center - radius
    iso_part = 0.5 * (jnp.maximum(upper, 0.0) + jnp.maximum(lower, 0.0))
    factor = jnp.clip(upper / (2.0 * jnp.maximum(radius, 0.05)), 0.0, 1.0)
    return iso_part + factor * spread, iso_part - factor * spread, factor * shear


def kernel(
    sectors,
    doms,
    strain_hbm,
    corner_hbm,
    counts_hbm,
    seam_hbm,
    velocity_hbm,
    dual_hbm,
    load_hbm,
    mobility_hbm,
    past_dual_hbm,
    past_dual_gap_hbm,
    past_velocity_hbm,
    past_velocity_gap_hbm,
    result,
    counts,
    strain,
    corner,
    velocity,
    dual,
    load,
    mobility,
    past_dual,
    past_dual_gap,
    past_velocity,
    past_velocity_gap,
    speed,
    load6,
    mob6,
    strain_r,
    own_seam,
    seam_in,
    base_out,
    base_in,
    own_out,
    own_in,
    seam_out,
    seam_part,
    seam_speed,
    speed_in,
    edge_in,
    force,
    force_in,
    push_in,
    onehot,
    lhs_far,
    lhs_near,
    lhs_own,
    gram_out,
    gram_in,
    total_out,
    total_in,
    mask_far,
    mask_near,
    load_sem,
    ready,
    send_sem,
    recv_sem,
):
    sec = lax.axis_index("sector")
    dom = lax.axis_index("dom")
    prev_sec = lax.rem(sec + sectors - 1, sectors)
    next_sec = lax.rem(sec + 1, sectors)
    left = lax.rem(dom + doms - 1, doms)
    right = lax.rem(dom + 1, doms)

    def copy(src, dst, sem, s, d):
        return pltpu.make_async_remote_copy(
            src_ref=src,
            dst_ref=dst,
            send_sem=send_sem.at[sem],
            recv_sem=recv_sem.at[sem],
            device_id=(s, d),
            device_id_type=MESH,
        )

    def far_first(k):
        step = (k + 1) // 2
        return lax.rem(dom + doms // 2 + jnp.where(lax.rem(k, 2) == 1, doms - step, step), doms)

    barrier = pltpu.get_barrier_semaphore()

    def signal(s, d):
        pl.semaphore_signal(barrier, inc=1, device_id=(s, d), device_id_type=MESH)

    chips = doms // 2
    reach = chips // 4
    chip, core = dom // 2, lax.rem(dom, 2)

    def at(offset, c):
        return 2 * lax.rem(chip + offset + chips, chips) + c

    def greet_sec(o, c):
        signal(lax.rem(sec + o, sectors), dom)
        return c

    loads = [
        pltpu.make_async_copy(src, dst, load_sem.at[i])
        for i, (src, dst) in enumerate(
            [
                (velocity_hbm, velocity),
                (load_hbm, load),
                (mobility_hbm, mobility),
                (corner_hbm, corner),
                (strain_hbm, strain),
                (dual_hbm, dual),
                (past_dual_gap_hbm, past_dual_gap),
                (past_velocity_gap_hbm, past_velocity_gap),
                (past_dual_hbm, past_dual),
                (past_velocity_hbm, past_velocity),
                (counts_hbm, counts),
                (seam_hbm, own_seam),
            ]
        )
    ]
    loads[0].start()
    for distance in range(reach, -1, -1):
        for offset in sorted({distance, -distance}):
            for c in range(2):
                signal(next_sec, at(offset, c))
                if distance > 0:
                    signal(sec, at(offset, c))
    signal(sec, at(0, 1 - core))
    lax.fori_loop(2, sectors - 1, greet_sec, 0)
    for l in loads[1:]:
        l.start()

    iota_row = lax.broadcasted_iota(jnp.int32, (8, LANES), 0)
    iota_lane = lax.broadcasted_iota(jnp.int32, (8, LANES), 1)

    speed[...] = jnp.zeros_like(speed)
    load6[...] = jnp.zeros_like(load6)
    for l in loads[0:3]:
        l.wait()
    for j in range(3):
        for h in range(2):
            r, cols = 2 * j + h, pl.ds(LANES * h, LANES)
            speed[0, r : r + 1, :] = velocity[j : j + 1, cols]
            load6[r : r + 1, :] = load[j : j + 1, cols]
    mob6[...] = jnp.where(
        lax.rem(iota_row, 2) == 0,
        jnp.broadcast_to(mobility[0:1, :], (8, LANES)),
        jnp.broadcast_to(mobility[1:2, :], (8, LANES)),
    )

    pl.semaphore_wait(barrier, 2 * (2 * reach + 1) + 4 * reach + 1 + (sectors - 3))

    six = pl.ds(0, 6)

    def send_edges(it):
        copy(speed.at[it, six], edge_in.at[it, 0, six], 1 + 2 * it, sec, right).start()
        copy(speed.at[it, six], edge_in.at[it, 1, six], 2 + 2 * it, sec, left).start()

    def wait_edges(it, what):
        getattr(copy(speed.at[it, six], edge_in.at[it, 0, six], 1 + 2 * it, sec, right), what)()
        getattr(copy(speed.at[it, six], edge_in.at[it, 1, six], 2 + 2 * it, sec, left), what)()

    def some_blocks(count, sem):
        block = speed_in.at[0, pl.ds(0, count), six]
        return copy(block, block, sem, prev_sec, dom)

    def relay_copy(offset, sem):
        return copy(speed.at[0, six], speed_in.at[0, dom, six], sem, prev_sec, at(offset, core))

    def send_first():
        def direct(offset, c):
            copy(speed.at[0, six], speed_in.at[0, dom, six], 0, prev_sec, at(offset, c)).start()

        relay_copy(reach, 6).start()
        relay_copy(-reach, 7).start()
        direct(reach, 1 - core)
        direct(-reach, 1 - core)
        for offset in range(reach - 1, -1, -1):
            for o in sorted({offset, -offset}):
                for c in range(2):
                    direct(o, c)
        send_edges(0)

    def pass_on():
        def forward(src, sem, offset, c):
            copy(speed_in.at[0, src, six], speed_in.at[0, src, six], sem, sec, at(offset, c)).start()

        def answer(offset):
            pl.semaphore_signal(ready, inc=1, device_id=(next_sec, at(offset, core)), device_id_type=MESH)

        relay_copy(reach, 6).wait_recv()
        answer(-reach)
        for m in range(reach, 0, -1):
            for c in range(2):
                forward(at(-reach, core), 8, m, c)
        relay_copy(-reach, 7).wait_recv()
        answer(reach)
        for m in range(reach - 1, 0, -1):
            for c in range(2):
                forward(at(reach, core), 8, -m, c)

    def wait_first():
        wait_edges(0, "wait_recv")
        some_blocks(4 * reach, 0).wait_recv()
        some_blocks(2 * (2 * reach - 1), 8).wait_recv()

    def wait_first_sends():
        wait_edges(0, "wait_send")
        relay_copy(reach, 6).wait_send()
        relay_copy(-reach, 7).wait_send()
        some_blocks(4 * reach, 0).wait_send()
        some_blocks(2 * (2 * reach - 1), 8).wait_send()

    def all_small(ref, count, sem):
        block = ref.at[pl.ds(0, count)]
        return copy(block, block, sem, sec, dom)

    def small_wait(i, what):
        ref, count, sem = [(base_in, doms, 18), (own_in, doms, 19), (seam_part, doms - 1, 20), (seam_speed, doms - 1, 9)][i]
        getattr(all_small(ref, count, sem), what)()

    def send_base(k, c):
        d = far_first(k)
        copy(base_out.at[d], base_in.at[dom], 18, prev_sec, d).start()
        return c

    def send_own(k, c):
        d = far_first(k)
        copy(own_out.at[d], own_in.at[dom], 19, prev_sec, d).start()
        return c

    def send_seam(k, c):
        d = far_first(k)
        copy(seam_out.at[d], seam_part.at[dom], 20, sec, d).start()
        return c

    def send_seam_speed(k, c):
        copy(seam_speed.at[dom], seam_speed.at[dom], 9, sec, far_first(k)).start()
        return c

    def wait_force(it, what="wait_recv"):
        getattr(copy(force.at[it, doms, six], push_in.at[it, 1, six], 12 + 2 * it, sec, left), what)()
        getattr(copy(force.at[it, doms + 1, six], push_in.at[it, 0, six], 13 + 2 * it, sec, right), what)()
        block = force_in.at[it, :, six]
        getattr(copy(block, block, 10 + it, next_sec, dom), what)()

    for offset in (reach, -reach):
        pl.semaphore_signal(ready, inc=1, device_id=(sec, at(offset, core)), device_id_type=MESH)

    seam_copy = copy(seam_hbm, seam_in, 5, prev_sec, dom)
    send_first()
    seam_copy.start()

    for l in loads[3:]:
        l.wait()
    for c in range(3):
        for j in range(3):
            for k in range(4):
                r = 12 * c + 3 * k + j
                for h in range(2):
                    strain_r[3 * c + j, 4 * h + k : 4 * h + k + 1, :] = strain[r : r + 1, pl.ds(LANES * h, LANES)]
    nodes = jnp.concatenate([corner[:, 0:LANES], corner[:, LANES : 2 * LANES]], axis=0)
    slot = LANES * (iota_row // 4) + iota_lane
    alive = jnp.where(slot < counts[0], 1.0, 0.0)
    dual_prev = [
        jnp.where(
            iota_row < 4,
            jnp.broadcast_to(dual[c : c + 1, 0:LANES], (8, LANES)),
            jnp.broadcast_to(dual[c : c + 1, LANES : 2 * LANES], (8, LANES)),
        )
        for c in range(3)
    ]

    pass_on()

    sector_nodes = doms * 2 * LANES
    seam_copy.wait_recv()
    position = nodes - sector_nodes
    place = jnp.bitwise_and(position, LANES - 1)
    place_row = jnp.right_shift(position, 7)
    seam_node = jnp.zeros((8, LANES), jnp.int32)
    for r in range(seam_in.shape[1] // LANES):
        row = jnp.broadcast_to(seam_in[0:1, LANES * r : LANES * (r + 1)], (8, LANES))
        seam_node = jnp.where(place_row == r, lane_take(row, place), seam_node)
    is_seam = position >= 0
    key = jnp.where(is_seam, 4 + jnp.right_shift(seam_node, 7), jnp.right_shift(nodes, 7) - 2 * dom + 1)
    low = jnp.bitwise_and(jnp.where(is_seam, seam_node, nodes), LANES - 1)

    lane_is = lax.broadcasted_iota(jnp.int32, (LANES, LANES), 0)
    for t in range(8):
        hit = lane_is == jnp.broadcast_to(low[t : t + 1, :], (LANES, LANES))
        onehot[:, LANES * t : LANES * (t + 1)] = jnp.where(hit, 1.0, 0.0).astype(jnp.bfloat16)

    half = doms // 2
    wanted = jnp.concatenate([row_bcast(key, t) - jnp.bitwise_and(iota_row, 1) for t in range(8)], axis=1)

    def mark(mask, q, keys):
        pair = jnp.concatenate([jnp.where(wanted == k, 1.0, 0.0) for k in keys], axis=0)
        mask[pl.ds(pl.multiple_of(16 * q, 16), 16), :] = pair.astype(jnp.bfloat16)

    def mark_far(q, c):
        mark(mask_far, q, [4 + 2 * far_first(2 * q + i) for i in range(2)])
        return c

    def mark_near(q, c):
        mark(mask_near, q, [4 + 2 * far_first(half + 2 * q + i) for i in range(2)])
        return c

    lax.fori_loop(0, half // 2, mark_far, 0)
    lax.fori_loop(0, half // 2, mark_near, 0)
    mark(mask_near, half // 2, [0, 2])

    low_half = iota_lane < LANES // 2
    groups = own_seam.shape[1] // (8 * LANES)

    def positions(ref, g):
        rows = [ref[0:1, LANES * (8 * g + r) : LANES * (8 * g + r + 1)] for r in range(8)]
        node = jnp.concatenate(rows, axis=0)
        return jnp.right_shift(node, 7), jnp.bitwise_and(node, LANES - 1)

    def swap(x):
        return pltpu.roll(x, LANES // 2, 1)

    def write_messages(ref, g, first, second, third, fourth):
        even = (jnp.where(low_half, first, swap(second)), jnp.where(low_half, third, swap(fourth)))
        odd = (jnp.where(low_half, swap(first), second), jnp.where(low_half, swap(third), fourth))
        for r in range(8):
            for parity, rows in enumerate((even, odd)):
                for i in range(2):
                    ref[2 * (8 * g + r) + parity, i : i + 1, :] = rows[i][r : r + 1, :]

    zero = jnp.zeros((8, LANES), jnp.float32)
    base6 = speed[0] + mob6[...] * load6[...]
    for g in range(groups):
        node_row, node_lane = positions(own_seam, g)
        found = [zero] * 4
        for h in range(2):
            hit = node_row == 2 * dom + h
            for j in range(4):
                row = row_bcast(base6, 2 * j + h) if j < 3 else row_bcast(mob6[...], h)
                found[j] = jnp.where(hit, lane_take(row, node_lane), found[j])
        write_messages(base_out, g, *found)

    def seam_forces():
        for g in range(groups):
            node_row, node_lane = positions(seam_in, g)
            found = [zero] * 3
            for k in range(doms):
                block = force[0, k]
                for h in range(2):
                    hit = node_row == 2 * far_first(k) + h
                    for j in range(3):
                        found[j] = jnp.where(hit, lane_take(row_bcast(block, 2 * j + h), node_lane), found[j])
            write_messages(seam_out, g, *found, zero)

    def own_forces():
        for g in range(groups):
            node_row, node_lane = positions(own_seam, g)
            found = [zero] * 3
            for row_key in range(4):
                block = force[0, doms + row_key // 2]
                hit = node_row - 2 * dom + 1 == row_key
                for j in range(3):
                    row = row_bcast(block, 2 * j + row_key % 2)
                    found[j] = jnp.where(hit, lane_take(row, node_lane), found[j])
            write_messages(own_out, g, *found, zero)

    def sum_blocks(refs):
        group = [ref[b] for ref in refs for b in range(doms)]
        while len(group) > 1:
            group = [x + y for x, y in zip(group[::2], group[1::2])] + group[len(group) - len(group) % 2 :]
        return group[0]

    def collect():
        seam_part[dom] = seam_out[dom]
        small_wait(0, "wait_recv")
        base = sum_blocks([base_in])
        half_lane = lax.broadcasted_iota(jnp.int32, (2, LANES), 1) < LANES // 2
        last = jnp.broadcast_to(base[1:2, :], (2, LANES))
        step = jnp.where(half_lane, pltpu.roll(last, LANES // 2, 1), last)
        small_wait(1, "wait_recv")
        small_wait(2, "wait_recv")
        seam_speed[dom] = base - step * sum_blocks([own_in, seam_part])
        lax.fori_loop(0, doms - 1, send_seam_speed, 0)

    collector = jnp.where(is_seam, jnp.right_shift(position, 6), -1)
    place_low = jnp.bitwise_and(position, LANES // 2 - 1)

    def elements(it, dual_now):
        def look(table, row_key, acc, h):
            out = []
            for j in range(3):
                row = jnp.broadcast_to(table[2 * j + h : 2 * j + h + 1, :], (8, LANES))
                out.append(jnp.where(key == row_key, lane_take(row, low), acc[j]))
            return out

        acc = [jnp.zeros((8, LANES), jnp.float32)] * 3
        acc = look(edge_in.at[it, 0], 0, acc, 1)
        acc = look(speed.at[it], 1, acc, 0)
        acc = look(speed.at[it], 2, acc, 1)
        acc = look(edge_in.at[it, 1], 3, acc, 0)

        for b in range(doms):
            if it == 0:
                acc = look(speed_in.at[it, b], 4 + 2 * b, acc, 0)
                acc = look(speed_in.at[it, b], 5 + 2 * b, acc, 1)
            else:
                hit = collector == b
                rows = [jnp.broadcast_to(seam_speed[b, i : i + 1, :], (8, LANES)) for i in range(2)]
                picks = [(rows[0], place_low), (rows[0], place_low + LANES // 2), (rows[1], place_low)]
                acc = [jnp.where(hit, lane_take(*pick), x) for pick, x in zip(picks, acc)]
        rate = []
        for c in range(3):
            part = strain_r[3 * c] * acc[0] + strain_r[3 * c + 1] * acc[1] + strain_r[3 * c + 2] * acc[2]
            rate.append(sum_corners(part, iota_row))
        trial = [rate[c] + dual_now[c] for c in range(3)]
        cone = project_cone(*trial)
        dual_next = [alive * (trial[c] - cone[c]) for c in range(3)]
        misfit = [alive * (rate[c] - cone[c] + dual_next[c]) for c in range(3)]
        push = [
            strain_r[j] * misfit[0] + strain_r[3 + j] * misfit[1] + strain_r[6 + j] * misfit[2] for j in range(3)
        ]
        return dual_next, push

    def spread(it, push):
        split = [[], [], []]
        for t in range(8):
            value = jnp.where(iota_row < 2, row_bcast(push[0], t), row_bcast(push[1], t))
            value = jnp.where(iota_row < 4, value, row_bcast(push[2], t))
            value = jnp.where(iota_row < 6, value, 0.0)
            for s in range(3):
                piece = value.astype(jnp.bfloat16).astype(jnp.float32)
                split[s].append(piece)
                value = value - piece
        split = [jnp.concatenate(p, axis=1) for p in split]
        split = [jnp.concatenate([p, p], axis=0).astype(jnp.bfloat16) for p in split]

        def fill(lhs, mask, first=0):
            for q in range(lhs.shape[1] // 16):
                rows = slice(16 * q, 16 * q + 16)
                hit = mask[first + 16 * q : first + 16 * q + 16, :]
                for s in range(3):
                    lhs[s, rows, :] = hit * split[s]

        def product(lhs):
            rows = lhs.shape[1]
            out = lax.dot_general(
                lhs[...].reshape(3 * rows, 8 * LANES),
                onehot[...],
                (((1,), (1,)), ((), ())),
                preferred_element_type=jnp.float32,
            ).reshape(3, rows // 8, 8, LANES)
            return (out[2] + out[1]) + out[0]

        def send(k, c):
            copy(force.at[it, k, six], force_in.at[it, dom, six], 10 + it, next_sec, far_first(k)).start()
            return c

        def send_pushes():
            copy(force.at[it, doms, six], push_in.at[it, 1, six], 12 + 2 * it, sec, left).start()
            copy(force.at[it, doms + 1, six], push_in.at[it, 0, six], 13 + 2 * it, sec, right).start()

        def spread_own():
            fill(lhs_own, mask_near, 4 * doms)
            force[it, doms : doms + 2] = product(lhs_own)

        def spread_half(lhs, mask, first):
            fill(lhs, mask)
            force[it, first : first + half] = product(lhs)

        if it == 0:
            spread_own()
            own_forces()
            lax.fori_loop(0, doms, send_own, 0)
            spread_half(lhs_far, mask_far, 0)
            spread_half(lhs_near, mask_near, half)
            seam_forces()
            lax.fori_loop(0, doms - 1, send_seam, 0)
            lax.fori_loop(0, doms, send, 0)
            send_pushes()
        else:
            spread_half(lhs_far, mask_far, 0)
            lax.fori_loop(0, half, send, 0)
            spread_half(lhs_near, mask_near, half)
            lax.fori_loop(half, doms, send, 0)
            spread_own()
            send_pushes()

    def next_speed(it):
        even = lax.rem(iota_row, 2) == 0
        own = jnp.where(
            even,
            pltpu.roll(force[it, doms] + jnp.where(iota_row < 6, push_in[it, 0], 0.0), 7, 0),
            pltpu.roll(force[it, doms + 1] + jnp.where(iota_row < 6, push_in[it, 1], 0.0), 1, 0),
        )

        for b in range(0, doms, 8):
            group = [force_in[it, b + i] for i in range(8)]
            while len(group) > 1:
                group = [x + y for x, y in zip(group[::2], group[1::2])]
            own = own + group[0]
        step = speed[it] - mob6[...] * (own - load6[...])
        return jnp.where(iota_row < 6, step, 0.0)

    wait_first()
    dual_one, push = elements(0, dual_prev)
    pl.semaphore_wait(ready, 4)
    lax.fori_loop(0, doms, send_base, 0)
    spread(0, push)
    collect()
    wait_force(0)
    speed[1] = next_speed(0)
    send_edges(1)
    wait_edges(1, "wait_recv")
    small_wait(3, "wait_recv")
    dual_two, push = elements(1, dual_one)
    spread(1, push)

    def by_history(ref, j, h):
        return ref[j, :, pl.ds(LANES * h, LANES)]

    depth = 8
    acc = [jnp.zeros((8, LANES), jnp.float32)] * (depth + 1)

    def add_gram(acc, res_row, past):
        res_b = jnp.broadcast_to(res_row, (8, LANES))
        gap = res_b - past
        acc = [acc[i] + gap * row_bcast(gap, i) for i in range(depth)] + [acc[depth] + gap * res_b]
        return acc

    for c in range(3):
        res = dual_two[c] - dual_one[c]
        for h in range(2):
            acc = add_gram(acc, res[4 * h : 4 * h + 1, :], by_history(past_dual_gap, c, h))

    wait_force(1)
    speed_one = speed[1]
    speed_two = next_speed(1)
    res = speed_two - speed_one
    for j in range(3):
        for h in range(2):
            r = 2 * j + h
            acc = add_gram(acc, res[r : r + 1, :], by_history(past_velocity_gap, j, h))
    packed = jnp.zeros((8, LANES), jnp.float32)
    for i in range(depth + 1):
        packed = jnp.where(iota_lane == i, jnp.sum(acc[i], axis=1, keepdims=True), packed)

    def fold(x):
        out = x[0:1, :]
        for l in range(1, 8):
            out = out + pltpu.roll(x[l : l + 1, :], 16 * l, 1)
        return out

    gram_out[0] = fold(packed)

    def send_gram(k, c):
        copy(gram_out.at[0], gram_in.at[k], 16, sec, far_first(k)).start()
        return c

    lax.fori_loop(0, doms - 1, send_gram, 0)
    block = gram_in.at[pl.ds(0, doms - 1)]
    gram_copies = copy(block, block, 16, sec, dom)
    gram_copies.wait_recv()

    def add_all(own, ref, first, last):
        group = [own] + [ref[o] for o in range(first, last)]
        while len(group) > 1:
            group = [x + y for x, y in zip(group[::2], group[1::2])] + group[len(group) - len(group) % 2 :]
        return group[0]

    total = add_all(gram_out[0], gram_in, 0, doms - 1)
    total_out[0] = total

    def steps(o):
        return min(o % 4, 4 - o % 4) + min(o // 4, sectors // 4 - o // 4)

    for o in sorted(range(1, sectors), key=steps, reverse=True):
        copy(total_out.at[0], total_in.at[o], 17, lax.rem(sec + o, sectors), dom).start()
    block = total_in.at[pl.ds(1, sectors - 1)]
    total_copies = copy(block, block, 17, sec, dom)

    def apart(now_row, past, past_gap):
        return jnp.broadcast_to(now_row, (8, LANES)) - past - past_gap

    parts = [(j, h) for j in range(3) for h in range(2)]
    apart_u = [
        apart(speed_two[2 * j + h : 2 * j + h + 1, :], by_history(past_velocity, j, h), by_history(past_velocity_gap, j, h))
        for j, h in parts
    ]
    apart_w = [
        apart(dual_two[j][4 * h : 4 * h + 1, :], by_history(past_dual, j, h), by_history(past_dual_gap, j, h))
        for j, h in parts
    ]
    seam_copy.wait_send()
    wait_first_sends()
    wait_edges(1, "wait_send")
    for i in range(4):
        small_wait(i, "wait_send")
    for it in range(ITERS):
        wait_force(it, "wait_send")
    gram_copies.wait_send()
    total_copies.wait_recv()

    total = add_all(total, total_in, 1, sectors)

    def entry(lane):
        return jnp.broadcast_to(jnp.broadcast_to(total[:, lane : lane + 1], (1, LANES)), (8, LANES))

    upper = [[entry(16 * i + l) if l >= i else None for l in range(depth + 1)] for i in range(depth)]
    trace = upper[0][0]
    for i in range(1, depth):
        trace = trace + upper[i][i]
    ridge = 0.0001 * trace / depth
    for i in range(depth):
        upper[i][i] = upper[i][i] + ridge
    inverse = []
    for k in range(depth):
        inverse.append(1.0 / upper[k][k])
        for i in range(k + 1, depth):
            scale = upper[k][i] * inverse[k]
            for l in range(i, depth + 1):
                upper[i][l] = upper[i][l] - scale * upper[k][l]
    solved = [None] * depth
    for k in reversed(range(depth)):
        value = upper[k][depth]
        for l in range(k + 1, depth):
            value = value - upper[k][l] * solved[l]
        solved[k] = value * inverse[k]
    coeffs = solved[0]
    for i in range(1, depth):
        coeffs = jnp.where(iota_row == i, solved[i], coeffs)

    for p, (j, h) in enumerate(parts):
        cols = pl.ds(LANES * h, LANES)
        result[j : j + 1, cols] = speed_two[2 * j + h : 2 * j + h + 1, :] - jnp.sum(
            coeffs * apart_u[p], axis=0, keepdims=True
        )
        result[4 + j : 5 + j, cols] = dual_two[j][4 * h : 4 * h + 1, :] - jnp.sum(
            coeffs * apart_w[p], axis=0, keepdims=True
        )
    total_copies.wait_send()


def per_device(
    strain_map,
    corner_nodes,
    counts,
    seam_nodes,
    velocity,
    dual_state,
    nodal_load,
    mobility,
    past_dual,
    past_dual_gap,
    past_velocity,
    past_velocity_gap,
):
    sectors, doms = lax.axis_size("sector"), lax.axis_size("dom")
    out = jax.ShapeDtypeStruct(velocity.shape, jnp.float32)
    vmem = pl.BlockSpec(memory_space=pltpu.VMEM)
    hbm = pl.BlockSpec(memory_space=pl.ANY)
    history = pltpu.VMEM((3, 8, 2 * LANES), jnp.float32)
    small = pltpu.VMEM((doms, 2, LANES), jnp.float32)
    f32 = jnp.float32
    result = pl.pallas_call(
        functools.partial(kernel, sectors, doms),
        out_shape=pltpu.VMEM((8, 2 * LANES), f32),
        in_specs=[hbm] * 12,
        out_specs=vmem,
        scratch_shapes=[
            pltpu.SMEM(counts.shape, jnp.int32),
            pltpu.VMEM(strain_map.shape, f32),
            pltpu.VMEM(corner_nodes.shape, jnp.int32),
            pltpu.VMEM(velocity.shape, f32),
            pltpu.VMEM(dual_state.shape, f32),
            pltpu.VMEM(nodal_load.shape, f32),
            pltpu.VMEM((2, LANES), f32),
            history,
            history,
            history,
            history,
            pltpu.VMEM((2, 8, LANES), f32),
            pltpu.VMEM((8, LANES), f32),
            pltpu.VMEM((8, LANES), f32),
            pltpu.VMEM((9, 8, LANES), f32),
            pltpu.VMEM(seam_nodes.shape, jnp.int32),
            pltpu.VMEM(seam_nodes.shape, jnp.int32),
            small,
            small,
            small,
            small,
            small,
            small,
            small,
            pltpu.VMEM((1, doms, 8, LANES), f32),
            pltpu.VMEM((2, 2, 8, LANES), f32),
            pltpu.VMEM((2, doms + 2, 8, LANES), f32),
            pltpu.VMEM((2, doms, 8, LANES), f32),
            pltpu.VMEM((2, 2, 8, LANES), f32),
            pltpu.VMEM((LANES, 8 * LANES), jnp.bfloat16),
            pltpu.VMEM((3, 4 * doms, 8 * LANES), jnp.bfloat16),
            pltpu.VMEM((3, 4 * doms, 8 * LANES), jnp.bfloat16),
            pltpu.VMEM((3, 16, 8 * LANES), jnp.bfloat16),
            pltpu.VMEM((1, 1, LANES), f32),
            pltpu.VMEM((doms, 1, LANES), f32),
            pltpu.VMEM((1, 1, LANES), f32),
            pltpu.VMEM((sectors, 1, LANES), f32),
            pltpu.VMEM((4 * doms, 8 * LANES), jnp.bfloat16),
            pltpu.VMEM((4 * doms + 16, 8 * LANES), jnp.bfloat16),
            pltpu.SemaphoreType.DMA((12,)),
            pltpu.SemaphoreType.REGULAR,
            pltpu.SemaphoreType.DMA((21,)),
            pltpu.SemaphoreType.DMA((21,)),
        ],
        compiler_params=pltpu.CompilerParams(collective_id=0, has_side_effects=True),
        name="dome",
    )(
        strain_map,
        corner_nodes,
        counts,
        seam_nodes,
        velocity,
        dual_state,
        nodal_load,
        mobility.reshape(2, LANES),
        past_dual.transpose(1, 0, 2),
        past_dual_gap.transpose(1, 0, 2),
        past_velocity.transpose(1, 0, 2),
        past_velocity_gap.transpose(1, 0, 2),
    )
    return result[0:3], result[4:7]


def solution(mesh):
    part = ("sector", "dom")
    in_specs = (
        P(None, part),
        P(None, part),
        P(part),
        P("sector", None),
        P(None, part),
        P(None, part),
        P(None, part),
        P(part),
        P(None, None, part),
        P(None, None, part),
        P(None, None, part),
        P(None, None, part),
    )
    out_specs = (P(None, part), P(None, part))
    return jax.shard_map(per_device, mesh=mesh, in_specs=in_specs, out_specs=out_specs, check_vma=False)
```

```python
import functools

import jax
import jax.numpy as jnp
from jax import lax
from jax.experimental import pallas as pl
from jax.experimental.pallas import tpu as pltpu
from jax.sharding import PartitionSpec as P

MESH = pl.DeviceIdType.MESH
ITERS = 2
LANES = 128


def row_bcast(x, r):
    return jnp.broadcast_to(x[r : r + 1, :], (8, LANES))


def lane_take(row, index):
    return jnp.take_along_axis(row, index, axis=1, mode="promise_in_bounds")


def sum_corners(x, iota_row):
    odd = lax.rem(iota_row, 2) == 1
    x = x + jnp.where(odd, pltpu.roll(x, 1, 0), pltpu.roll(x, 7, 0))
    high = lax.rem(iota_row, 4) >= 2
    return x + jnp.where(high, pltpu.roll(x, 2, 0), pltpu.roll(x, 6, 0))


def project_cone(a, b, shear):
    center = 0.5 * (a + b)
    spread = 0.5 * (a - b)
    radius = jnp.sqrt(spread * spread + shear * shear)
    upper = center + radius
    lower = center - radius
    iso_part = 0.5 * (jnp.maximum(upper, 0.0) + jnp.maximum(lower, 0.0))
    factor = jnp.clip(upper / (2.0 * jnp.maximum(radius, 0.05)), 0.0, 1.0)
    return iso_part + factor * spread, iso_part - factor * spread, factor * shear


def kernel(
    sectors,
    doms,
    strain_hbm,
    corner_hbm,
    counts_hbm,
    seam_hbm,
    velocity_hbm,
    dual_hbm,
    load_hbm,
    mobility_hbm,
    past_dual_hbm,
    past_dual_gap_hbm,
    past_velocity_hbm,
    past_velocity_gap_hbm,
    result,
    counts,
    strain,
    corner,
    velocity,
    dual,
    load,
    mobility,
    past_dual,
    past_dual_gap,
    past_velocity,
    past_velocity_gap,
    speed,
    load6,
    mob6,
    strain_r,
    own_seam,
    seam_in,
    base_out,
    base_in,
    own_out,
    own_in,
    seam_out,
    seam_part,
    seam_speed,
    speed_in,
    edge_in,
    force,
    force_in,
    push_in,
    onehot,
    lhs_far,
    lhs_near,
    lhs_own,
    gram_out,
    gram_in,
    total_out,
    total_in,
    mask_far,
    mask_near,
    load_sem,
    ready,
    send_sem,
    recv_sem,
):
    sec = lax.axis_index("sector")
    dom = lax.axis_index("dom")
    prev_sec = lax.rem(sec + sectors - 1, sectors)
    next_sec = lax.rem(sec + 1, sectors)
    left = lax.rem(dom + doms - 1, doms)
    right = lax.rem(dom + 1, doms)

    def copy(src, dst, sem, s, d):
        return pltpu.make_async_remote_copy(
            src_ref=src,
            dst_ref=dst,
            send_sem=send_sem.at[sem],
            recv_sem=recv_sem.at[sem],
            device_id=(s, d),
            device_id_type=MESH,
        )

    def far_first(k):
        step = (k + 1) // 2
        return lax.rem(dom + doms // 2 + jnp.where(lax.rem(k, 2) == 1, doms - step, step), doms)

    barrier = pltpu.get_barrier_semaphore()

    def signal(s, d):
        pl.semaphore_signal(barrier, inc=1, device_id=(s, d), device_id_type=MESH)

    chips = doms // 2
    reach = chips // 4
    chip, core = dom // 2, lax.rem(dom, 2)

    def at(offset, c):
        return 2 * lax.rem(chip + offset + chips, chips) + c

    def greet_sec(o, c):
        signal(lax.rem(sec + o, sectors), dom)
        return c

    loads = [
        pltpu.make_async_copy(src, dst, load_sem.at[i])
        for i, (src, dst) in enumerate(
            [
                (velocity_hbm, velocity),
                (load_hbm, load),
                (mobility_hbm, mobility),
                (corner_hbm, corner),
                (strain_hbm, strain),
                (dual_hbm, dual),
                (past_dual_gap_hbm, past_dual_gap),
                (past_velocity_gap_hbm, past_velocity_gap),
                (past_dual_hbm, past_dual),
                (past_velocity_hbm, past_velocity),
                (counts_hbm, counts),
                (seam_hbm, own_seam),
            ]
        )
    ]
    loads[0].start()
    for distance in range(reach, -1, -1):
        for offset in sorted({distance, -distance}):
            for c in range(2):
                signal(next_sec, at(offset, c))
                if distance > 0:
                    signal(sec, at(offset, c))
    signal(sec, at(0, 1 - core))
    lax.fori_loop(2, sectors - 1, greet_sec, 0)
    for l in loads[1:]:
        l.start()

    iota_row = lax.broadcasted_iota(jnp.int32, (8, LANES), 0)
    iota_lane = lax.broadcasted_iota(jnp.int32, (8, LANES), 1)

    speed[...] = jnp.zeros_like(speed)
    load6[...] = jnp.zeros_like(load6)
    for l in loads[0:3]:
        l.wait()
    for j in range(3):
        for h in range(2):
            r, cols = 2 * j + h, pl.ds(LANES * h, LANES)
            speed[0, r : r + 1, :] = velocity[j : j + 1, cols]
            load6[r : r + 1, :] = load[j : j + 1, cols]
    mob6[...] = jnp.where(
        lax.rem(iota_row, 2) == 0,
        jnp.broadcast_to(mobility[0:1, :], (8, LANES)),
        jnp.broadcast_to(mobility[1:2, :], (8, LANES)),
    )

    pl.semaphore_wait(barrier, 2 * (2 * reach + 1) + 4 * reach + 1 + (sectors - 3))

    six = pl.ds(0, 6)

    def send_edges(it):
        copy(speed.at[it, six], edge_in.at[it, 0, six], 1 + 2 * it, sec, right).start()
        copy(speed.at[it, six], edge_in.at[it, 1, six], 2 + 2 * it, sec, left).start()

    def wait_edges(it, what):
        getattr(copy(speed.at[it, six], edge_in.at[it, 0, six], 1 + 2 * it, sec, right), what)()
        getattr(copy(speed.at[it, six], edge_in.at[it, 1, six], 2 + 2 * it, sec, left), what)()

    def some_blocks(count, sem):
        block = speed_in.at[0, pl.ds(0, count), six]
        return copy(block, block, sem, prev_sec, dom)

    def relay_copy(offset, sem):
        return copy(speed.at[0, six], speed_in.at[0, dom, six], sem, prev_sec, at(offset, core))

    def send_first():
        def direct(offset, c):
            copy(speed.at[0, six], speed_in.at[0, dom, six], 0, prev_sec, at(offset, c)).start()

        relay_copy(reach, 6).start()
        relay_copy(-reach, 7).start()
        direct(reach, 1 - core)
        direct(-reach, 1 - core)
        for offset in range(reach - 1, -1, -1):
            for o in sorted({offset, -offset}):
                for c in range(2):
                    direct(o, c)
        send_edges(0)

    def pass_on():
        def forward(src, sem, offset, c):
            copy(speed_in.at[0, src, six], speed_in.at[0, src, six], sem, sec, at(offset, c)).start()

        def answer(offset):
            pl.semaphore_signal(ready, inc=1, device_id=(next_sec, at(offset, core)), device_id_type=MESH)

        relay_copy(reach, 6).wait_recv()
        answer(-reach)
        for m in range(reach, 0, -1):
            for c in range(2):
                forward(at(-reach, core), 8, m, c)
        relay_copy(-reach, 7).wait_recv()
        answer(reach)
        for m in range(reach - 1, 0, -1):
            for c in range(2):
                forward(at(reach, core), 8, -m, c)

    def wait_first():
        wait_edges(0, "wait_recv")
        some_blocks(4 * reach, 0).wait_recv()
        some_blocks(2 * (2 * reach - 1), 8).wait_recv()

    def wait_first_sends():
        wait_edges(0, "wait_send")
        relay_copy(reach, 6).wait_send()
        relay_copy(-reach, 7).wait_send()
        some_blocks(4 * reach, 0).wait_send()
        some_blocks(2 * (2 * reach - 1), 8).wait_send()

    def all_small(ref, count, sem):
        block = ref.at[pl.ds(0, count)]
        return copy(block, block, sem, sec, dom)

    def small_wait(i, what):
        ref, count, sem = [(base_in, doms, 18), (own_in, doms, 19), (seam_part, doms - 1, 20), (seam_speed, doms - 1, 9)][i]
        getattr(all_small(ref, count, sem), what)()

    def send_base(k, c):
        d = far_first(k)
        copy(base_out.at[d], base_in.at[dom], 18, prev_sec, d).start()
        return c

    def send_own(k, c):
        d = far_first(k)
        copy(own_out.at[d], own_in.at[dom], 19, prev_sec, d).start()
        return c

    def send_seam(k, c):
        d = far_first(k)
        copy(seam_out.at[d], seam_part.at[dom], 20, sec, d).start()
        return c

    def send_seam_speed(k, c):
        copy(seam_speed.at[dom], seam_speed.at[dom], 9, sec, far_first(k)).start()
        return c

    def wait_force(it, what="wait_recv"):
        getattr(copy(force.at[it, doms, six], push_in.at[it, 1, six], 12 + 2 * it, sec, left), what)()
        getattr(copy(force.at[it, doms + 1, six], push_in.at[it, 0, six], 13 + 2 * it, sec, right), what)()
        block = force_in.at[it, :, six]
        getattr(copy(block, block, 10 + it, next_sec, dom), what)()

    for offset in (reach, -reach):
        pl.semaphore_signal(ready, inc=1, device_id=(sec, at(offset, core)), device_id_type=MESH)

    seam_copy = copy(seam_hbm, seam_in, 5, prev_sec, dom)
    send_first()
    seam_copy.start()

    for l in loads[3:]:
        l.wait()
    for c in range(3):
        for j in range(3):
            for k in range(4):
                r = 12 * c + 3 * k + j
                for h in range(2):
                    strain_r[3 * c + j, 4 * h + k : 4 * h + k + 1, :] = strain[r : r + 1, pl.ds(LANES * h, LANES)]
    nodes = jnp.concatenate([corner[:, 0:LANES], corner[:, LANES : 2 * LANES]], axis=0)
    slot = LANES * (iota_row // 4) + iota_lane
    alive = jnp.where(slot < counts[0], 1.0, 0.0)
    dual_prev = [
        jnp.where(
            iota_row < 4,
            jnp.broadcast_to(dual[c : c + 1, 0:LANES], (8, LANES)),
            jnp.broadcast_to(dual[c : c + 1, LANES : 2 * LANES], (8, LANES)),
        )
        for c in range(3)
    ]

    pass_on()

    sector_nodes = doms * 2 * LANES
    seam_copy.wait_recv()
    position = nodes - sector_nodes
    place = jnp.bitwise_and(position, LANES - 1)
    place_row = jnp.right_shift(position, 7)
    seam_node = jnp.zeros((8, LANES), jnp.int32)
    for r in range(seam_in.shape[1] // LANES):
        row = jnp.broadcast_to(seam_in[0:1, LANES * r : LANES * (r + 1)], (8, LANES))
        seam_node = jnp.where(place_row == r, lane_take(row, place), seam_node)
    is_seam = position >= 0
    key = jnp.where(is_seam, 4 + jnp.right_shift(seam_node, 7), jnp.right_shift(nodes, 7) - 2 * dom + 1)
    low = jnp.bitwise_and(jnp.where(is_seam, seam_node, nodes), LANES - 1)

    lane_is = lax.broadcasted_iota(jnp.int32, (LANES, LANES), 0)
    for t in range(8):
        hit = lane_is == jnp.broadcast_to(low[t : t + 1, :], (LANES, LANES))
        onehot[:, LANES * t : LANES * (t + 1)] = jnp.where(hit, 1.0, 0.0).astype(jnp.bfloat16)

    half = doms // 2
    wanted = jnp.concatenate([row_bcast(key, t) - jnp.bitwise_and(iota_row, 1) for t in range(8)], axis=1)

    def mark(mask, q, keys):
        pair = jnp.concatenate([jnp.where(wanted == k, 1.0, 0.0) for k in keys], axis=0)
        mask[pl.ds(pl.multiple_of(16 * q, 16), 16), :] = pair.astype(jnp.bfloat16)

    def mark_far(q, c):
        mark(mask_far, q, [4 + 2 * far_first(2 * q + i) for i in range(2)])
        return c

    def mark_near(q, c):
        mark(mask_near, q, [4 + 2 * far_first(half + 2 * q + i) for i in range(2)])
        return c

    lax.fori_loop(0, half // 2, mark_far, 0)
    lax.fori_loop(0, half // 2, mark_near, 0)
    mark(mask_near, half // 2, [0, 2])

    low_half = iota_lane < LANES // 2
    groups = own_seam.shape[1] // (8 * LANES)

    def positions(ref, g):
        rows = [ref[0:1, LANES * (8 * g + r) : LANES * (8 * g + r + 1)] for r in range(8)]
        node = jnp.concatenate(rows, axis=0)
        return jnp.right_shift(node, 7), jnp.bitwise_and(node, LANES - 1)

    def swap(x):
        return pltpu.roll(x, LANES // 2, 1)

    def write_messages(ref, g, first, second, third, fourth):
        even = (jnp.where(low_half, first, swap(second)), jnp.where(low_half, third, swap(fourth)))
        odd = (jnp.where(low_half, swap(first), second), jnp.where(low_half, swap(third), fourth))
        for r in range(8):
            for parity, rows in enumerate((even, odd)):
                for i in range(2):
                    ref[2 * (8 * g + r) + parity, i : i + 1, :] = rows[i][r : r + 1, :]

    zero = jnp.zeros((8, LANES), jnp.float32)
    base6 = speed[0] + mob6[...] * load6[...]
    for g in range(groups):
        node_row, node_lane = positions(own_seam, g)
        found = [zero] * 4
        for h in range(2):
            hit = node_row == 2 * dom + h
            for j in range(4):
                row = row_bcast(base6, 2 * j + h) if j < 3 else row_bcast(mob6[...], h)
                found[j] = jnp.where(hit, lane_take(row, node_lane), found[j])
        write_messages(base_out, g, *found)

    def seam_forces():
        for g in range(groups):
            node_row, node_lane = positions(seam_in, g)
            found = [zero] * 3
            for k in range(doms):
                block = force[0, k]
                for h in range(2):
                    hit = node_row == 2 * far_first(k) + h
                    for j in range(3):
                        found[j] = jnp.where(hit, lane_take(row_bcast(block, 2 * j + h), node_lane), found[j])
            write_messages(seam_out, g, *found, zero)

    def own_forces():
        for g in range(groups):
            node_row, node_lane = positions(own_seam, g)
            found = [zero] * 3
            for row_key in range(4):
                block = force[0, doms + row_key // 2]
                hit = node_row - 2 * dom + 1 == row_key
                for j in range(3):
                    row = row_bcast(block, 2 * j + row_key % 2)
                    found[j] = jnp.where(hit, lane_take(row, node_lane), found[j])
            write_messages(own_out, g, *found, zero)

    def sum_blocks(refs):
        group = [ref[b] for ref in refs for b in range(doms)]
        while len(group) > 1:
            group = [x + y for x, y in zip(group[::2], group[1::2])] + group[len(group) - len(group) % 2 :]
        return group[0]

    def collect():
        seam_part[dom] = seam_out[dom]
        small_wait(0, "wait_recv")
        base = sum_blocks([base_in])
        half_lane = lax.broadcasted_iota(jnp.int32, (2, LANES), 1) < LANES // 2
        last = jnp.broadcast_to(base[1:2, :], (2, LANES))
        step = jnp.where(half_lane, pltpu.roll(last, LANES // 2, 1), last)
        small_wait(1, "wait_recv")
        small_wait(2, "wait_recv")
        seam_speed[dom] = base - step * sum_blocks([own_in, seam_part])
        lax.fori_loop(0, doms - 1, send_seam_speed, 0)

    collector = jnp.where(is_seam, jnp.right_shift(position, 6), -1)
    place_low = jnp.bitwise_and(position, LANES // 2 - 1)

    def elements(it, dual_now):
        def look(table, row_key, acc, h):
            out = []
            for j in range(3):
                row = jnp.broadcast_to(table[2 * j + h : 2 * j + h + 1, :], (8, LANES))
                out.append(jnp.where(key == row_key, lane_take(row, low), acc[j]))
            return out

        acc = [jnp.zeros((8, LANES), jnp.float32)] * 3
        acc = look(edge_in.at[it, 0], 0, acc, 1)
        acc = look(speed.at[it], 1, acc, 0)
        acc = look(speed.at[it], 2, acc, 1)
        acc = look(edge_in.at[it, 1], 3, acc, 0)

        for b in range(doms):
            if it == 0:
                acc = look(speed_in.at[it, b], 4 + 2 * b, acc, 0)
                acc = look(speed_in.at[it, b], 5 + 2 * b, acc, 1)
            else:
                hit = collector == b
                rows = [jnp.broadcast_to(seam_speed[b, i : i + 1, :], (8, LANES)) for i in range(2)]
                picks = [(rows[0], place_low), (rows[0], place_low + LANES // 2), (rows[1], place_low)]
                acc = [jnp.where(hit, lane_take(*pick), x) for pick, x in zip(picks, acc)]
        rate = []
        for c in range(3):
            part = strain_r[3 * c] * acc[0] + strain_r[3 * c + 1] * acc[1] + strain_r[3 * c + 2] * acc[2]
            rate.append(sum_corners(part, iota_row))
        trial = [rate[c] + dual_now[c] for c in range(3)]
        cone = project_cone(*trial)
        dual_next = [alive * (trial[c] - cone[c]) for c in range(3)]
        misfit = [alive * (rate[c] - cone[c] + dual_next[c]) for c in range(3)]
        push = [
            strain_r[j] * misfit[0] + strain_r[3 + j] * misfit[1] + strain_r[6 + j] * misfit[2] for j in range(3)
        ]
        return dual_next, push

    def spread(it, push):
        split = [[], [], []]
        for t in range(8):
            value = jnp.where(iota_row < 2, row_bcast(push[0], t), row_bcast(push[1], t))
            value = jnp.where(iota_row < 4, value, row_bcast(push[2], t))
            value = jnp.where(iota_row < 6, value, 0.0)
            for s in range(3):
                piece = value.astype(jnp.bfloat16).astype(jnp.float32)
                split[s].append(piece)
                value = value - piece
        split = [jnp.concatenate(p, axis=1) for p in split]
        split = [jnp.concatenate([p, p], axis=0).astype(jnp.bfloat16) for p in split]

        def fill(lhs, mask, first=0):
            for q in range(lhs.shape[1] // 16):
                rows = slice(16 * q, 16 * q + 16)
                hit = mask[first + 16 * q : first + 16 * q + 16, :]
                for s in range(3):
                    lhs[s, rows, :] = hit * split[s]

        def product(lhs):
            rows = lhs.shape[1]
            out = lax.dot_general(
                lhs[...].reshape(3 * rows, 8 * LANES),
                onehot[...],
                (((1,), (1,)), ((), ())),
                preferred_element_type=jnp.float32,
            ).reshape(3, rows // 8, 8, LANES)
            return (out[2] + out[1]) + out[0]

        def send(k, c):
            copy(force.at[it, k, six], force_in.at[it, dom, six], 10 + it, next_sec, far_first(k)).start()
            return c

        def send_pushes():
            copy(force.at[it, doms, six], push_in.at[it, 1, six], 12 + 2 * it, sec, left).start()
            copy(force.at[it, doms + 1, six], push_in.at[it, 0, six], 13 + 2 * it, sec, right).start()

        def spread_own():
            fill(lhs_own, mask_near, 4 * doms)
            force[it, doms : doms + 2] = product(lhs_own)

        def spread_half(lhs, mask, first):
            fill(lhs, mask)
            force[it, first : first + half] = product(lhs)

        if it == 0:
            spread_own()
            own_forces()
            lax.fori_loop(0, doms, send_own, 0)
            spread_half(lhs_far, mask_far, 0)
            spread_half(lhs_near, mask_near, half)
            seam_forces()
            lax.fori_loop(0, doms - 1, send_seam, 0)
            lax.fori_loop(0, doms, send, 0)
            send_pushes()
        else:
            quarter = half // 2
            for q in range(2):
                rows = pl.ds(8 * quarter * q, 8 * quarter)
                fill(lhs_far.at[:, rows], mask_far, 8 * quarter * q)
                force[it, quarter * q : quarter * (q + 1)] = product(lhs_far.at[:, rows])
                lax.fori_loop(quarter * q, quarter * (q + 1), send, 0)
            spread_half(lhs_near, mask_near, half)
            lax.fori_loop(half, doms, send, 0)
            spread_own()
            send_pushes()

    def next_speed(it):
        even = lax.rem(iota_row, 2) == 0
        own = jnp.where(
            even,
            pltpu.roll(force[it, doms] + jnp.where(iota_row < 6, push_in[it, 0], 0.0), 7, 0),
            pltpu.roll(force[it, doms + 1] + jnp.where(iota_row < 6, push_in[it, 1], 0.0), 1, 0),
        )

        for b in range(0, doms, 8):
            group = [force_in[it, b + i] for i in range(8)]
            while len(group) > 1:
                group = [x + y for x, y in zip(group[::2], group[1::2])]
            own = own + group[0]
        step = speed[it] - mob6[...] * (own - load6[...])
        return jnp.where(iota_row < 6, step, 0.0)

    lax.fori_loop(half, doms, send_base, 0)
    wait_first()
    dual_one, push = elements(0, dual_prev)
    pl.semaphore_wait(ready, 4)
    lax.fori_loop(0, half, send_base, 0)
    spread(0, push)
    collect()
    wait_force(0)
    speed[1] = next_speed(0)
    send_edges(1)
    wait_edges(1, "wait_recv")
    small_wait(3, "wait_recv")
    dual_two, push = elements(1, dual_one)
    spread(1, push)

    def by_history(ref, j, h):
        return ref[j, :, pl.ds(LANES * h, LANES)]

    depth = 8
    acc = [jnp.zeros((8, LANES), jnp.float32)] * (depth + 1)

    def add_gram(acc, res_row, past):
        res_b = jnp.broadcast_to(res_row, (8, LANES))
        gap = res_b - past
        acc = [acc[i] + gap * row_bcast(gap, i) for i in range(depth)] + [acc[depth] + gap * res_b]
        return acc

    for c in range(3):
        res = dual_two[c] - dual_one[c]
        for h in range(2):
            acc = add_gram(acc, res[4 * h : 4 * h + 1, :], by_history(past_dual_gap, c, h))

    wait_force(1)
    speed_one = speed[1]
    speed_two = next_speed(1)
    res = speed_two - speed_one
    for j in range(3):
        for h in range(2):
            r = 2 * j + h
            acc = add_gram(acc, res[r : r + 1, :], by_history(past_velocity_gap, j, h))
    packed = jnp.zeros((8, LANES), jnp.float32)
    for i in range(depth + 1):
        packed = jnp.where(iota_lane == i, jnp.sum(acc[i], axis=1, keepdims=True), packed)

    def fold(x):
        out = x[0:1, :]
        for l in range(1, 8):
            out = out + pltpu.roll(x[l : l + 1, :], 16 * l, 1)
        return out

    gram_out[0] = fold(packed)

    def send_gram(k, c):
        copy(gram_out.at[0], gram_in.at[k], 16, sec, far_first(k)).start()
        return c

    lax.fori_loop(0, doms - 1, send_gram, 0)
    block = gram_in.at[pl.ds(0, doms - 1)]
    gram_copies = copy(block, block, 16, sec, dom)
    gram_copies.wait_recv()

    def add_all(own, ref, first, last):
        group = [own] + [ref[o] for o in range(first, last)]
        while len(group) > 1:
            group = [x + y for x, y in zip(group[::2], group[1::2])] + group[len(group) - len(group) % 2 :]
        return group[0]

    total = add_all(gram_out[0], gram_in, 0, doms - 1)
    total_out[0] = total

    def steps(o):
        return min(o % 4, 4 - o % 4) + min(o // 4, sectors // 4 - o // 4)

    for o in sorted(range(1, sectors), key=steps, reverse=True):
        copy(total_out.at[0], total_in.at[o], 17, lax.rem(sec + o, sectors), dom).start()
    block = total_in.at[pl.ds(1, sectors - 1)]
    total_copies = copy(block, block, 17, sec, dom)

    def apart(now_row, past, past_gap):
        return jnp.broadcast_to(now_row, (8, LANES)) - past - past_gap

    parts = [(j, h) for j in range(3) for h in range(2)]
    apart_u = [
        apart(speed_two[2 * j + h : 2 * j + h + 1, :], by_history(past_velocity, j, h), by_history(past_velocity_gap, j, h))
        for j, h in parts
    ]
    apart_w = [
        apart(dual_two[j][4 * h : 4 * h + 1, :], by_history(past_dual, j, h), by_history(past_dual_gap, j, h))
        for j, h in parts
    ]
    seam_copy.wait_send()
    wait_first_sends()
    wait_edges(1, "wait_send")
    for i in range(4):
        small_wait(i, "wait_send")
    for it in range(ITERS):
        wait_force(it, "wait_send")
    gram_copies.wait_send()
    total_copies.wait_recv()

    total = add_all(total, total_in, 1, sectors)

    def entry(lane):
        return jnp.broadcast_to(jnp.broadcast_to(total[:, lane : lane + 1], (1, LANES)), (8, LANES))

    upper = [[entry(16 * i + l) if l >= i else None for l in range(depth + 1)] for i in range(depth)]
    trace = upper[0][0]
    for i in range(1, depth):
        trace = trace + upper[i][i]
    ridge = 0.0001 * trace / depth
    for i in range(depth):
        upper[i][i] = upper[i][i] + ridge
    inverse = []
    for k in range(depth):
        inverse.append(1.0 / upper[k][k])
        for i in range(k + 1, depth):
            scale = upper[k][i] * inverse[k]
            for l in range(i, depth + 1):
                upper[i][l] = upper[i][l] - scale * upper[k][l]
    solved = [None] * depth
    for k in reversed(range(depth)):
        value = upper[k][depth]
        for l in range(k + 1, depth):
            value = value - upper[k][l] * solved[l]
        solved[k] = value * inverse[k]
    coeffs = solved[0]
    for i in range(1, depth):
        coeffs = jnp.where(iota_row == i, solved[i], coeffs)

    for p, (j, h) in enumerate(parts):
        cols = pl.ds(LANES * h, LANES)
        result[j : j + 1, cols] = speed_two[2 * j + h : 2 * j + h + 1, :] - jnp.sum(
            coeffs * apart_u[p], axis=0, keepdims=True
        )
        result[4 + j : 5 + j, cols] = dual_two[j][4 * h : 4 * h + 1, :] - jnp.sum(
            coeffs * apart_w[p], axis=0, keepdims=True
        )
    total_copies.wait_send()


def per_device(
    strain_map,
    corner_nodes,
    counts,
    seam_nodes,
    velocity,
    dual_state,
    nodal_load,
    mobility,
    past_dual,
    past_dual_gap,
    past_velocity,
    past_velocity_gap,
):
    sectors, doms = lax.axis_size("sector"), lax.axis_size("dom")
    out = jax.ShapeDtypeStruct(velocity.shape, jnp.float32)
    vmem = pl.BlockSpec(memory_space=pltpu.VMEM)
    hbm = pl.BlockSpec(memory_space=pl.ANY)
    history = pltpu.VMEM((3, 8, 2 * LANES), jnp.float32)
    small = pltpu.VMEM((doms, 2, LANES), jnp.float32)
    f32 = jnp.float32
    result = pl.pallas_call(
        functools.partial(kernel, sectors, doms),
        out_shape=pltpu.VMEM((8, 2 * LANES), f32),
        in_specs=[hbm] * 12,
        out_specs=vmem,
        scratch_shapes=[
            pltpu.SMEM(counts.shape, jnp.int32),
            pltpu.VMEM(strain_map.shape, f32),
            pltpu.VMEM(corner_nodes.shape, jnp.int32),
            pltpu.VMEM(velocity.shape, f32),
            pltpu.VMEM(dual_state.shape, f32),
            pltpu.VMEM(nodal_load.shape, f32),
            pltpu.VMEM((2, LANES), f32),
            history,
            history,
            history,
            history,
            pltpu.VMEM((2, 8, LANES), f32),
            pltpu.VMEM((8, LANES), f32),
            pltpu.VMEM((8, LANES), f32),
            pltpu.VMEM((9, 8, LANES), f32),
            pltpu.VMEM(seam_nodes.shape, jnp.int32),
            pltpu.VMEM(seam_nodes.shape, jnp.int32),
            small,
            small,
            small,
            small,
            small,
            small,
            small,
            pltpu.VMEM((1, doms, 8, LANES), f32),
            pltpu.VMEM((2, 2, 8, LANES), f32),
            pltpu.VMEM((2, doms + 2, 8, LANES), f32),
            pltpu.VMEM((2, doms, 8, LANES), f32),
            pltpu.VMEM((2, 2, 8, LANES), f32),
            pltpu.VMEM((LANES, 8 * LANES), jnp.bfloat16),
            pltpu.VMEM((3, 4 * doms, 8 * LANES), jnp.bfloat16),
            pltpu.VMEM((3, 4 * doms, 8 * LANES), jnp.bfloat16),
            pltpu.VMEM((3, 16, 8 * LANES), jnp.bfloat16),
            pltpu.VMEM((1, 1, LANES), f32),
            pltpu.VMEM((doms, 1, LANES), f32),
            pltpu.VMEM((1, 1, LANES), f32),
            pltpu.VMEM((sectors, 1, LANES), f32),
            pltpu.VMEM((4 * doms, 8 * LANES), jnp.bfloat16),
            pltpu.VMEM((4 * doms + 16, 8 * LANES), jnp.bfloat16),
            pltpu.SemaphoreType.DMA((12,)),
            pltpu.SemaphoreType.REGULAR,
            pltpu.SemaphoreType.DMA((21,)),
            pltpu.SemaphoreType.DMA((21,)),
        ],
        compiler_params=pltpu.CompilerParams(collective_id=0, has_side_effects=True),
        name="dome",
    )(
        strain_map,
        corner_nodes,
        counts,
        seam_nodes,
        velocity,
        dual_state,
        nodal_load,
        mobility.reshape(2, LANES),
        past_dual.transpose(1, 0, 2),
        past_dual_gap.transpose(1, 0, 2),
        past_velocity.transpose(1, 0, 2),
        past_velocity_gap.transpose(1, 0, 2),
    )
    return result[0:3], result[4:7]


def solution(mesh):
    part = ("sector", "dom")
    in_specs = (
        P(None, part),
        P(None, part),
        P(part),
        P("sector", None),
        P(None, part),
        P(None, part),
        P(None, part),
        P(part),
        P(None, None, part),
        P(None, None, part),
        P(None, None, part),
        P(None, None, part),
    )
    out_specs = (P(None, part), P(None, part))
    return jax.shard_map(per_device, mesh=mesh, in_specs=in_specs, out_specs=out_specs, check_vma=False)
```
